32 devices in a mesh: slab: 2 (over x), page: 16 (over z, y, core).
Axes of the slice: x: 2, y: 2, z: 4, core: 2. Of those that a mesh axis runs over, the one named last changes fastest.
Arguments:
- latents: bfloat16 [128, 1024], P(('slab', 'page')), parts along dimension 0, may hold values from -6 to 6
- patches: bfloat16 [65536, 1024], P(('slab', 'page')), parts along dimension 0, may hold values from -6 to 6
- lat_gain: float32 [1024], replicated, may hold values from 0.1 to 1.9
- patch_gain: float32 [1024], replicated, may hold values from 0.1 to 1.9
- mlp_gain: float32 [1024], replicated, may hold values from 0.1 to 1.9
- w_query: bfloat16 [1024, 1024], replicated, may hold values from -0.5 to 0.5
- w_key: bfloat16 [1024, 1024], replicated, may hold values from -0.1875 to 0.1875
- w_value: bfloat16 [1024, 1024], replicated, may hold values from -0.1875 to 0.1875
- w_out: bfloat16 [1024, 1024], replicated, may hold values from -0.5 to 0.5
- w_hidden: bfloat16 [1024, 4096], P(None, 'page'), may hold values from -0.1875 to 0.1875
- w_connect: bfloat16 [4096, 4096], P(None, 'page'), may hold values from -0.09375 to 0.09375
Outputs:
- resampled: bfloat16 [128, 1024], P(('slab', 'page')), parts along dimension 0
- connector: bfloat16 [128, 4096], P('slab', 'page'), parts along dimension 0
The draws below stay inside these ranges and needn't reach their ends.
There are 2 independent parts, one for each index of `slab`. The reference program is written for one: setup_inputs(seed, part) draws one part's arguments, and reference() takes and returns one part's arrays. A program takes and returns all parts, laid end to end along the dimension named above; an argument that names none is the same for every part. Nothing has to cross between parts.
All inputs are finite; a program needn't handle non-finite values.
Results may differ from the reference program's by a relative error of at most 0.012.
Values may be sent and summed in bfloat16 or wider, within the bound.
No kernel may reach another device: no remote copies, remote signals or barrier semaphores. Data moves between devices by JAX's collectives and lax.ppermute only.
A program may use at most 128 MiB of HBM per device.

```python
import math
import jax
import jax.numpy as jnp
from jax import lax

D = 1024
HEADS = 16
FF = 4096
OUT = 4096
PATCH_DEV = 2048
HEAD_DIM = 64
NL = 64
PATCHES = 32768
N_PAGE = 16


def block_scale(stream_key, dims, cuts, smallest, top_value):
    factor_of = 1.0
    for dim, blocks in cuts:
        heights = jax.random.uniform(jax.random.fold_in(jax.random.fold_in(stream_key, 6), dim), (blocks,), jnp.float32, smallest / len(cuts), top_value / len(cuts))
        factor_of = factor_of * jnp.repeat(jnp.exp(heights), dims[dim] // blocks).reshape((-1,) + (1,) * (len(dims) - 1 - dim))
    return factor_of


def gaussian(own_key, extent, deviation, bound, shards=(), held_as=jnp.bfloat16):
    values = jax.random.normal(own_key, extent, jnp.float32) * deviation
    if len(shards) > 0:
        values = block_scale(own_key, extent, shards, -0.22, 0.18) * values
    return jnp.clip(values, min=-bound, max=bound).astype(held_as)


def setup_inputs(seed: int = 0, part: int = 0) -> dict:
    streams_of = jax.random.split(jax.random.key(seed), 12)
    own_keys = jax.random.split(jax.random.fold_in(streams_of[11], part), 12)
    latents = gaussian(own_keys[0], (NL, D), 1.0, 6.0, ((0, 16),))
    patches = gaussian(own_keys[1], (PATCHES, D), 1.0, 6.0, ((0, 16),))
    lat_gain = jnp.clip(1.0 + 0.18 * jax.random.normal(streams_of[2], (D,), jnp.float32), 0.1, 1.9)
    patch_gain = jnp.clip(1.0 + 0.18 * jax.random.normal(streams_of[3], (D,), jnp.float32), 0.1, 1.9)
    mlp_gain = jnp.clip(1.0 + 0.18 * jax.random.normal(streams_of[4], (D,), jnp.float32), 0.1, 1.9)
    w_query = gaussian(streams_of[5], (D, D), (D // 8) ** -0.5, 0.5)
    w_key = gaussian(streams_of[6], (D, D), D ** -0.5, 0.1875)
    w_value = gaussian(streams_of[7], (D, D), D ** -0.5, 0.1875)
    w_out = gaussian(streams_of[8], (D, D), (D // 8) ** -0.5, 0.5)
    w_hidden = gaussian(streams_of[9], (D, FF), D ** -0.5, 0.1875, ((1, 16),))
    w_connect = gaussian(streams_of[10], (FF, OUT), FF ** -0.5, 0.09375, ((1, 16),))
    return {"latents": latents, "patches": patches, "lat_gain": lat_gain, "patch_gain": patch_gain, "mlp_gain": mlp_gain, "w_query": w_query, "w_key": w_key, "w_value": w_value, "w_out": w_out, "w_hidden": w_hidden, "w_connect": w_connect}


def norm_rows(values_in, gain):
    center = values_in - lax.optimization_barrier(jnp.mean(values_in, axis=-1, keepdims=True))
    spread = lax.optimization_barrier(jnp.mean(center * center, axis=-1, keepdims=True))
    return center * lax.rsqrt(spread + 1e-05) * gain.astype(jnp.float32)

def round_back(values_in):
    return lax.optimization_barrier(values_in.astype(jnp.bfloat16)).astype(jnp.float32)

def reference(latents, patches, lat_gain, patch_gain, mlp_gain, w_query, w_key, w_value, w_out, w_hidden, w_connect):
    lat_norm = norm_rows(latents.astype(jnp.float32), lat_gain).astype(jnp.bfloat16)
    query = jnp.dot(lat_norm, w_query, preferred_element_type=jnp.float32)
    query_heads = round_back(query).reshape(NL, HEADS, HEAD_DIM)
    scale = 1.0 / math.sqrt(HEAD_DIM)
    blocks = patches.reshape(N_PAGE, PATCH_DEV, D)

    def visit(running, block_rows):
        numer, denom = running
        patch_norm = norm_rows(block_rows.astype(jnp.float32), patch_gain).astype(jnp.bfloat16)
        keys = round_back(jnp.dot(patch_norm, w_key, preferred_element_type=jnp.float32)).reshape(PATCH_DEV, HEADS, HEAD_DIM)
        values = round_back(jnp.dot(patch_norm, w_value, preferred_element_type=jnp.float32)).reshape(PATCH_DEV, HEADS, HEAD_DIM)
        scores = jnp.einsum('lhd,phd->hlp', query_heads, keys) * scale
        expo = jnp.exp(scores)
        denom = denom + lax.optimization_barrier(jnp.sum(expo, axis=-1))
        probs = round_back(expo)
        numer = numer + jnp.einsum('hlp,phd->lhd', probs, values)
        return ((numer, denom), None)
    start = (jnp.zeros((NL, HEADS, HEAD_DIM), jnp.float32), jnp.zeros((HEADS, NL), jnp.float32))
    (numer, denom), _ = lax.scan(visit, start, blocks)
    attended = (numer / jnp.transpose(denom)[:, :, None]).reshape(NL, D).astype(jnp.bfloat16)
    mixed = latents.astype(jnp.float32) + jnp.dot(attended, w_out, preferred_element_type=jnp.float32)
    resampled = mixed.astype(jnp.bfloat16)
    mlp_in = norm_rows(mixed, mlp_gain).astype(jnp.bfloat16)
    hidden = jax.nn.gelu(jnp.dot(mlp_in, w_hidden, preferred_element_type=jnp.float32), approximate=True).astype(jnp.bfloat16)
    connector = jnp.dot(hidden, w_connect, preferred_element_type=jnp.float32).astype(jnp.bfloat16)
    return (resampled, connector)
```

```python
import math

import jax
import jax.numpy as jnp
from jax import lax
from jax.experimental import pallas as pl
from jax.experimental.pallas import tpu as pltpu
from jax.sharding import PartitionSpec as P

HEADS = 16
PACK = 4
LANES = 128


def norm_rows(values_in, gain):
    center = values_in - jnp.mean(values_in, axis=-1, keepdims=True)
    spread = jnp.mean(center * center, axis=-1, keepdims=True)
    return center * lax.rsqrt(spread + 1e-05) * gain


def attend_kernel(x_ref, gain_ref, wk_ref, wv_ref, q_ref, num_ref, den_ref, qbd, acc, dacc):
    step = pl.program_id(0)
    block = x_ref.shape[0]
    latents, width = q_ref.shape
    head_dim = width // HEADS
    span = PACK * head_dim
    groups = HEADS // PACK
    lane_head = lax.broadcasted_iota(jnp.int32, (latents, span), 1) // head_dim

    @pl.when(step == 0)
    def _():
        acc[...] = jnp.zeros_like(acc)
        dacc[...] = jnp.zeros_like(dacc)
        for g in range(groups):
            part = q_ref[:, g * span : (g + 1) * span]
            for h in range(PACK):
                qbd[g, h * latents : (h + 1) * latents, :] = jnp.where(
                    lane_head == h, part, jnp.zeros_like(part)
                )

    x = x_ref[...].astype(jnp.float32)
    pn = norm_rows(x, gain_ref[...]).astype(jnp.bfloat16)
    keys = jnp.dot(pn, wk_ref[...], preferred_element_type=jnp.float32).astype(jnp.bfloat16)
    values = jnp.dot(pn, wv_ref[...], preferred_element_type=jnp.float32).astype(jnp.bfloat16)
    factor = math.log2(math.e) / math.sqrt(head_dim)
    for g in range(groups):
        cols = slice(g * span, (g + 1) * span)
        scores = lax.dot_general(
            qbd[g], keys[:, cols], (((1,), (1,)), ((), ())), preferred_element_type=jnp.float32
        )
        expo = jnp.exp2(scores * factor)
        total = expo[:, :LANES]
        for j in range(1, block // LANES):
            total = total + expo[:, j * LANES : (j + 1) * LANES]
        dacc[g] += total
        acc[g] += jnp.dot(
            expo.astype(jnp.bfloat16), values[:, cols], preferred_element_type=jnp.float32
        )

    @pl.when(step == pl.num_programs(0) - 1)
    def _():
        lane = lax.broadcasted_iota(jnp.int32, (latents, LANES), 1)
        out = jnp.zeros((latents, LANES), jnp.float32)
        for g in range(groups):
            sums = jnp.sum(dacc[g], axis=-1, keepdims=True)
            picked = jnp.zeros((latents, span), jnp.float32)
            for h in range(PACK):
                rows = slice(h * latents, (h + 1) * latents)
                picked = jnp.where(lane_head == h, acc[g, rows, :], picked)
                out = jnp.where(lane == g * PACK + h, sums[rows], out)
            num_ref[:, g * span : (g + 1) * span] = picked
        den_ref[...] = out


def attend(patches, gain, w_key, w_value, query):
    rows, width = patches.shape
    latents = query.shape[0]
    block = 256
    span = PACK * (width // HEADS)
    groups = HEADS // PACK
    whole = lambda shape: pl.BlockSpec(shape, lambda i: (0,) * len(shape))
    once = lambda shape: pl.BlockSpec(
        shape, lambda i: (0,) * len(shape), pipeline_mode=pl.Buffered(1)
    )
    return pl.pallas_call(
        attend_kernel,
        grid=(rows // block,),
        in_specs=[
            pl.BlockSpec((block, width), lambda i: (i, 0)),
            once((1, width)),
            once((width, width)),
            once((width, width)),
            once((latents, width)),
        ],
        out_specs=[whole((latents, width)), whole((latents, LANES))],
        out_shape=[
            jax.ShapeDtypeStruct((latents, width), jnp.float32),
            jax.ShapeDtypeStruct((latents, LANES), jnp.float32),
        ],
        scratch_shapes=[
            pltpu.VMEM((groups, PACK * latents, span), jnp.bfloat16),
            pltpu.VMEM((groups, PACK * latents, span), jnp.float32),
            pltpu.VMEM((groups, PACK * latents, LANES), jnp.float32),
        ],
        compiler_params=pltpu.CompilerParams(
            dimension_semantics=("arbitrary",), vmem_limit_bytes=48 * 1024 * 1024
        ),
        cost_estimate=pl.CostEstimate(
            flops=4 * rows * width * width + 4 * rows * latents * PACK * width,
            transcendentals=rows * latents * HEADS,
            bytes_accessed=2 * rows * width + 4 * width * width,
        ),
        name="attend",
    )(patches, gain.reshape(1, width), w_key, w_value, query)


def spread_rows(block, count):
    everyone = jnp.broadcast_to(block[None], (count,) + block.shape)
    return lax.all_to_all(everyone, "page", 0, 0, tiled=True)


def body(
    latents,
    patches,
    lat_gain,
    patch_gain,
    mlp_gain,
    w_query,
    w_key,
    w_value,
    w_out,
    w_hidden,
    w_connect,
):
    count = lax.axis_size("page")
    lat_rows, width = latents.shape
    head_dim = width // HEADS
    lat_norm = norm_rows(latents.astype(jnp.float32), lat_gain).astype(jnp.bfloat16)
    query = jnp.dot(lat_norm, w_query, preferred_element_type=jnp.float32).astype(jnp.bfloat16)
    query_all = spread_rows(query, count).reshape(count * lat_rows, width)
    numer, denom = attend(patches, patch_gain, w_key, w_value, query_all)
    packed = jnp.concatenate([numer, denom], axis=1).reshape(count, lat_rows, width + LANES)
    summed = jnp.sum(lax.all_to_all(packed, "page", 0, 0, tiled=True), axis=0)
    attended = (
        (summed[:, :width].reshape(lat_rows, HEADS, head_dim) / summed[:, width : width + HEADS, None])
        .reshape(lat_rows, width)
        .astype(jnp.bfloat16)
    )
    mixed = latents.astype(jnp.float32) + jnp.dot(
        attended, w_out, preferred_element_type=jnp.float32
    )
    resampled = mixed.astype(jnp.bfloat16)
    mlp_in = norm_rows(mixed, mlp_gain).astype(jnp.bfloat16)
    mlp_all = spread_rows(mlp_in, count).reshape(count * lat_rows, width)
    hidden = jax.nn.gelu(
        jnp.dot(mlp_all, w_hidden, preferred_element_type=jnp.float32), approximate=True
    ).astype(jnp.bfloat16)
    units = hidden.shape[1]
    hidden_all = spread_rows(hidden, count)
    connector = lax.dot_general(
        jnp.transpose(hidden_all, (1, 0, 2)).reshape(hidden.shape[0], count * units),
        w_connect,
        (((1,), (0,)), ((), ())),
        preferred_element_type=jnp.float32,
    ).astype(jnp.bfloat16)
    return (resampled, connector)


def solution(mesh):
    placed = (
        P(("slab", "page"), None),
        P(("slab", "page"), None),
        P(),
        P(),
        P(),
        P(),
        P(),
        P(),
        P(),
        P(None, "page"),
        P(None, "page"),
    )
    return jax.shard_map(
        body,
        mesh=mesh,
        in_specs=placed,
        out_specs=(P(("slab", "page"), None), P("slab", "page")),
        check_vma=False,
    )
```

```python
import math

import jax
import jax.numpy as jnp
from jax import lax
from jax.experimental import pallas as pl
from jax.experimental.pallas import tpu as pltpu
from jax.sharding import PartitionSpec as P

HEADS = 16
PACK = 4
LANES = 128
MIB = 1024 * 1024


def norm_rows(values_in, gain):
    center = values_in - jnp.mean(values_in, axis=-1, keepdims=True)
    spread = jnp.mean(center * center, axis=-1, keepdims=True)
    return center * lax.rsqrt(spread + 1e-05) * gain


def in_hbm(array):
    return pltpu.with_memory_space_constraint(array, pltpu.HBM)


def fixed(shape):
    return pl.BlockSpec(shape, lambda i: (0,) * len(shape), pipeline_mode=pl.Buffered(1))


def project_kernel(x_ref, gain_ref, wk_ref, wv_ref, k_ref, v_ref):
    x = x_ref[...].astype(jnp.float32)
    pn = norm_rows(x, gain_ref[...]).astype(jnp.bfloat16)
    k_ref[...] = jnp.dot(pn, wk_ref[...], preferred_element_type=jnp.float32).astype(jnp.bfloat16)
    v_ref[...] = jnp.dot(pn, wv_ref[...], preferred_element_type=jnp.float32).astype(jnp.bfloat16)


def project(patches, gain, w_key, w_value):
    rows, width = patches.shape
    block = math.gcd(rows, 512)
    tile = pl.BlockSpec((block, width), lambda i: (i, 0))
    return pl.pallas_call(
        project_kernel,
        grid=(rows // block,),
        in_specs=[tile, fixed((1, width)), fixed((width, width)), fixed((width, width))],
        out_specs=[tile, tile],
        out_shape=[pltpu.HBM((rows, width), jnp.bfloat16)] * 2,
        compiler_params=pltpu.CompilerParams(
            dimension_semantics=("arbitrary",), vmem_limit_bytes=26 * MIB
        ),
        cost_estimate=pl.CostEstimate(
            flops=4 * rows * width * width,
            transcendentals=rows,
            bytes_accessed=6 * rows * width + 4 * width * width,
        ),
        name="project",
    )(in_hbm(patches), gain.reshape(1, width), in_hbm(w_key), in_hbm(w_value))


def attend_kernel(lat_ref, gain_ref, wq_ref, k_ref, v_ref, out_ref, qbd, acc, dacc):
    step = pl.program_id(0)
    block = k_ref.shape[0]
    latents, width = lat_ref.shape
    head_dim = width // HEADS
    span = PACK * head_dim
    groups = HEADS // PACK
    lane_head = lax.broadcasted_iota(jnp.int32, (latents, span), 1) // head_dim

    @pl.when(step == 0)
    def _():
        acc[...] = jnp.zeros_like(acc)
        dacc[...] = jnp.zeros_like(dacc)
        lat_norm = norm_rows(lat_ref[...].astype(jnp.float32), gain_ref[...]).astype(jnp.bfloat16)
        query = jnp.dot(lat_norm, wq_ref[...], preferred_element_type=jnp.float32)
        for g in range(groups):
            part = query[:, g * span : (g + 1) * span]
            for h in range(PACK):
                qbd[g, h * latents : (h + 1) * latents, :] = jnp.where(
                    lane_head == h, part, jnp.zeros_like(part)
                ).astype(jnp.bfloat16)

    factor = math.log2(math.e) / math.sqrt(head_dim)
    for g in range(groups):
        cols = slice(g * span, (g + 1) * span)
        scores = lax.dot_general(
            qbd[g], k_ref[:, cols], (((1,), (1,)), ((), ())), preferred_element_type=jnp.float32
        )
        expo = jnp.exp2(scores * factor)
        total = expo[:, :LANES]
        for j in range(1, block // LANES):
            total = total + expo[:, j * LANES : (j + 1) * LANES]
        dacc[g] += total
        acc[g] += jnp.dot(
            expo.astype(jnp.bfloat16), v_ref[:, cols], preferred_element_type=jnp.float32
        )

    @pl.when(step == pl.num_programs(0) - 1)
    def _():
        lane = lax.broadcasted_iota(jnp.int32, (latents, LANES), 1)
        out = jnp.zeros((latents, LANES), jnp.float32)
        for g in range(groups):
            sums = jnp.sum(dacc[g], axis=-1, keepdims=True)
            high = sums.astype(jnp.bfloat16).astype(jnp.float32)
            low = sums - high
            picked = jnp.zeros((latents, span), jnp.float32)
            for h in range(PACK):
                rows = slice(h * latents, (h + 1) * latents)
                picked = jnp.where(lane_head == h, acc[g, rows, :], picked)
                out = jnp.where(lane == g * PACK + h, high[rows], out)
                out = jnp.where(lane == HEADS + g * PACK + h, low[rows], out)
            out_ref[:, g * span : (g + 1) * span] = picked.astype(jnp.bfloat16)
        out_ref[:, width:] = out.astype(jnp.bfloat16)


def attend(latents, gain, w_query, keys, values):
    rows, width = keys.shape
    count = latents.shape[0]
    block = math.gcd(rows, 512)
    span = PACK * (width // HEADS)
    groups = HEADS // PACK
    tile = pl.BlockSpec((block, width), lambda i: (i, 0))
    return pl.pallas_call(
        attend_kernel,
        grid=(rows // block,),
        in_specs=[fixed((count, width)), fixed((1, width)), fixed((width, width)), tile, tile],
        out_specs=pl.BlockSpec((count, width + LANES), lambda i: (0, 0)),
        out_shape=jax.ShapeDtypeStruct((count, width + LANES), jnp.bfloat16),
        scratch_shapes=[
            pltpu.VMEM((groups, PACK * count, span), jnp.bfloat16),
            pltpu.VMEM((groups, PACK * count, span), jnp.float32),
            pltpu.VMEM((groups, PACK * count, LANES), jnp.float32),
        ],
        compiler_params=pltpu.CompilerParams(
            dimension_semantics=("arbitrary",), vmem_limit_bytes=44 * MIB
        ),
        cost_estimate=pl.CostEstimate(
            flops=4 * rows * count * PACK * width,
            transcendentals=rows * count * HEADS,
            bytes_accessed=4 * rows * width + 2 * width * width,
        ),
        name="attend",
    )(latents, gain.reshape(1, width), in_hbm(w_query), in_hbm(keys), in_hbm(values))


def mix_kernel(parts_ref, lat_ref, wo_ref, gain_ref, res_ref, mlp_ref):
    rows, width = lat_ref.shape
    head_dim = width // HEADS
    total = parts_ref[0].astype(jnp.float32)
    for j in range(1, parts_ref.shape[0]):
        total = total + parts_ref[j].astype(jnp.float32)
    denom = total[:, width : width + HEADS] + total[:, width + HEADS : width + 2 * HEADS]
    wide = jnp.concatenate(
        [jnp.broadcast_to(denom[:, h : h + 1], (rows, head_dim)) for h in range(HEADS)], axis=1
    )
    attended = (total[:, :width] / wide).astype(jnp.bfloat16)
    mixed = lat_ref[...].astype(jnp.float32) + jnp.dot(
        attended, wo_ref[...], preferred_element_type=jnp.float32
    )
    res_ref[...] = mixed.astype(jnp.bfloat16)
    mlp_ref[...] = norm_rows(mixed, gain_ref[...]).astype(jnp.bfloat16)


def mix(parts, latents, w_out, gain):
    rows, width = latents.shape
    return pl.pallas_call(
        mix_kernel,
        out_shape=[jax.ShapeDtypeStruct((rows, width), jnp.bfloat16)] * 2,
        cost_estimate=pl.CostEstimate(
            flops=2 * rows * width * width,
            transcendentals=rows,
            bytes_accessed=2 * width * width + 2 * parts.size,
        ),
        name="mix",
    )(parts, latents, w_out, gain.reshape(1, width))


def spread_rows(block, count):
    everyone = jnp.broadcast_to(block[None], (count,) + block.shape)
    return lax.all_to_all(everyone, "page", 0, 0, tiled=True)


def spread_pairs(block, count):
    chips = count // 2
    sides = [[2 * chip + side for chip in range(chips)] for side in range(2)]
    everyone = jnp.broadcast_to(block[None], (chips,) + block.shape)
    mine = lax.all_to_all(everyone, "page", 0, 0, axis_index_groups=sides, tiled=True)
    theirs = lax.ppermute(mine, "page", [(i, i ^ 1) for i in range(count)])
    return mine, theirs


def body(
    latents,
    patches,
    lat_gain,
    patch_gain,
    mlp_gain,
    w_query,
    w_key,
    w_value,
    w_out,
    w_hidden,
    w_connect,
):
    count = lax.axis_size("page")
    lat_rows, width = latents.shape
    lat_all = spread_rows(latents, count).reshape(count * lat_rows, width)
    keys, values = project(patches, patch_gain, w_key, w_value)
    packed = attend(lat_all, lat_gain, w_query, keys, values)
    parts = lax.all_to_all(
        packed.reshape(count, lat_rows, width + LANES), "page", 0, 0, tiled=True
    )
    resampled, mlp_in = mix(parts, latents, w_out, mlp_gain)
    mlp_all = spread_rows(mlp_in, count).reshape(count * lat_rows, width)
    hidden = jax.nn.gelu(
        jnp.dot(mlp_all, w_hidden, preferred_element_type=jnp.float32), approximate=True
    ).astype(jnp.bfloat16)
    rows, units = hidden.shape
    mine, theirs = spread_pairs(hidden, count)
    even = lax.axis_index("page") % 2 == 0
    both = jnp.stack([jnp.where(even, mine, theirs), jnp.where(even, theirs, mine)], axis=1)
    hidden_all = jnp.transpose(both.reshape(count, rows, units), (1, 0, 2)).reshape(
        rows, count * units
    )
    connector = jnp.dot(hidden_all, w_connect, preferred_element_type=jnp.float32).astype(
        jnp.bfloat16
    )
    return (resampled, connector)


def solution(mesh):
    placed = (
        P(("slab", "page"), None),
        P(("slab", "page"), None),
        P(),
        P(),
        P(),
        P(),
        P(),
        P(),
        P(),
        P(None, "page"),
        P(None, "page"),
    )
    return jax.shard_map(
        body,
        mesh=mesh,
        in_specs=placed,
        out_specs=(P(("slab", "page"), None), P("slab", "page")),
        check_vma=False,
    )
```

```python
import math

import jax
import jax.numpy as jnp
from jax import lax
from jax.experimental import pallas as pl
from jax.experimental.pallas import tpu as pltpu
from jax.sharding import PartitionSpec as P

HEADS = 16
PACK = 4
LANES = 128
CHUNKS = 4
MIB = 1024 * 1024


def norm_rows(values_in, gain):
    center = values_in - jnp.mean(values_in, axis=-1, keepdims=True)
    spread = jnp.mean(center * center, axis=-1, keepdims=True)
    return center * lax.rsqrt(spread + 1e-05) * gain


def in_hbm(array):
    return pltpu.with_memory_space_constraint(array, pltpu.HBM)


def fixed(shape):
    return pl.BlockSpec(shape, lambda i: (0,) * len(shape), pipeline_mode=pl.Buffered(1))


def project_kernel(
    x_hbm, gain_ref, wk_hbm, wv_hbm, k_hbm, v_hbm, xs, wk, wv, ks, vs, pns, x_sem, w_sem, out_sem
):
    blocks, block, _ = xs.shape

    def fetch(i):
        return pltpu.make_async_copy(x_hbm.at[pl.ds(i * block, block)], xs.at[i], x_sem.at[i])

    def put(src, dst, which, i):
        return pltpu.make_async_copy(
            src.at[i], dst.at[pl.ds(i * block, block)], out_sem.at[which, i]
        )

    def normed(i):
        return norm_rows(xs[i].astype(jnp.float32), gain_ref[...]).astype(jnp.bfloat16)

    def times(weight, i):
        return jnp.dot(pns[i % 2], weight[...], preferred_element_type=jnp.float32).astype(
            jnp.bfloat16
        )

    key_copy = pltpu.make_async_copy(wk_hbm, wk, w_sem.at[0])
    value_copy = pltpu.make_async_copy(wv_hbm, wv, w_sem.at[1])
    fetch(0).start()
    key_copy.start()
    for i in range(1, min(2, blocks)):
        fetch(i).start()
    value_copy.start()
    for i in range(2, blocks):
        fetch(i).start()
    fetch(0).wait()
    pns[0] = normed(0)
    key_copy.wait()
    for i in range(blocks):
        ks[i] = times(wk, i)
        put(ks, k_hbm, 0, i).start()
        if i == 0:
            value_copy.wait()
        if i + 1 < blocks:
            fetch(i + 1).wait()
            pns[(i + 1) % 2] = normed(i + 1)
        vs[i] = times(wv, i)
        put(vs, v_hbm, 1, i).start()
    for i in range(blocks):
        put(ks, k_hbm, 0, i).wait()
        put(vs, v_hbm, 1, i).wait()


def project(patches, gain, w_key, w_value):
    rows, width = patches.shape
    block = math.gcd(rows, 512)
    blocks = rows // block
    hbm = pl.BlockSpec(memory_space=pltpu.HBM)
    return pl.pallas_call(
        project_kernel,
        in_specs=[hbm, pl.BlockSpec(memory_space=pltpu.VMEM), hbm, hbm],
        out_specs=[hbm, hbm],
        out_shape=[pltpu.HBM((rows, width), jnp.bfloat16)] * 2,
        scratch_shapes=[
            pltpu.VMEM((blocks, block, width), jnp.bfloat16),
            pltpu.VMEM((width, width), jnp.bfloat16),
            pltpu.VMEM((width, width), jnp.bfloat16),
            pltpu.VMEM((blocks, block, width), jnp.bfloat16),
            pltpu.VMEM((blocks, block, width), jnp.bfloat16),
            pltpu.VMEM((2, block, width), jnp.bfloat16),
            pltpu.SemaphoreType.DMA((blocks,)),
            pltpu.SemaphoreType.DMA((2,)),
            pltpu.SemaphoreType.DMA((2, blocks)),
        ],
        compiler_params=pltpu.CompilerParams(vmem_limit_bytes=32 * MIB),
        cost_estimate=pl.CostEstimate(
            flops=4 * rows * width * width,
            transcendentals=rows,
            bytes_accessed=6 * rows * width + 4 * width * width,
        ),
        name="project",
    )(in_hbm(patches), gain.reshape(1, width), in_hbm(w_key), in_hbm(w_value))


def attend_kernel(q_ref, k_ref, v_ref, out_ref, qbd, acc, dacc):
    step = pl.program_id(0)
    block = k_ref.shape[0]
    latents, width = q_ref.shape
    head_dim = width // HEADS
    span = PACK * head_dim
    groups = HEADS // PACK
    lane_head = lax.broadcasted_iota(jnp.int32, (latents, span), 1) // head_dim

    @pl.when(step == 0)
    def _():
        acc[...] = jnp.zeros_like(acc)
        dacc[...] = jnp.zeros_like(dacc)
        for g in range(groups):
            part = q_ref[:, g * span : (g + 1) * span]
            for h in range(PACK):
                qbd[g, h * latents : (h + 1) * latents, :] = jnp.where(
                    lane_head == h, part, jnp.zeros_like(part)
                )

    factor = math.log2(math.e) / math.sqrt(head_dim)
    for g in range(groups):
        cols = slice(g * span, (g + 1) * span)
        scores = lax.dot_general(
            qbd[g], k_ref[:, cols], (((1,), (1,)), ((), ())), preferred_element_type=jnp.float32
        )
        expo = jnp.exp2(scores * factor)
        total = expo[:, :LANES]
        for j in range(1, block // LANES):
            total = total + expo[:, j * LANES : (j + 1) * LANES]
        dacc[g] += total
        acc[g] += jnp.dot(
            expo.astype(jnp.bfloat16), v_ref[:, cols], preferred_element_type=jnp.float32
        )

    @pl.when(step == pl.num_programs(0) - 1)
    def _():
        lane = lax.broadcasted_iota(jnp.int32, (latents, LANES), 1)
        out = jnp.zeros((latents, LANES), jnp.float32)
        for g in range(groups):
            sums = jnp.sum(dacc[g], axis=-1, keepdims=True)
            high = sums.astype(jnp.bfloat16).astype(jnp.float32)
            low = sums - high
            picked = jnp.zeros((latents, span), jnp.float32)
            for h in range(PACK):
                rows = slice(h * latents, (h + 1) * latents)
                picked = jnp.where(lane_head == h, acc[g, rows, :], picked)
                out = jnp.where(lane == g * PACK + h, high[rows], out)
                out = jnp.where(lane == HEADS + g * PACK + h, low[rows], out)
            out_ref[:, g * span : (g + 1) * span] = picked.astype(jnp.bfloat16)
        out_ref[:, width:] = out.astype(jnp.bfloat16)


def attend(query, keys, values):
    rows, width = keys.shape
    count = query.shape[0]
    block = math.gcd(rows, 512)
    span = PACK * (width // HEADS)
    groups = HEADS // PACK
    tile = pl.BlockSpec((block, width), lambda i: (i, 0))
    return pl.pallas_call(
        attend_kernel,
        grid=(rows // block,),
        in_specs=[fixed((count, width)), tile, tile],
        out_specs=pl.BlockSpec((count, width + LANES), lambda i: (0, 0)),
        out_shape=jax.ShapeDtypeStruct((count, width + LANES), jnp.bfloat16),
        scratch_shapes=[
            pltpu.VMEM((groups, PACK * count, span), jnp.bfloat16),
            pltpu.VMEM((groups, PACK * count, span), jnp.float32),
            pltpu.VMEM((groups, PACK * count, LANES), jnp.float32),
        ],
        compiler_params=pltpu.CompilerParams(
            dimension_semantics=("arbitrary",), vmem_limit_bytes=30 * MIB
        ),
        cost_estimate=pl.CostEstimate(
            flops=4 * rows * count * PACK * width,
            transcendentals=rows * count * HEADS,
            bytes_accessed=4 * rows * width,
        ),
        name="attend",
    )(query, in_hbm(keys), in_hbm(values))


def start_chunks(hbm, chunks, sem):
    size = chunks.shape[1]
    fetches = [
        pltpu.make_async_copy(hbm.at[pl.ds(i * size, size)], chunks.at[i], sem.at[i])
        for i in range(chunks.shape[0])
    ]
    for fetch in fetches:
        fetch.start()
    return fetches


def times_chunks(rows, fetches, chunks, total):
    size = chunks.shape[1]
    for i, fetch in enumerate(fetches):
        fetch.wait()
        part = jnp.dot(
            rows[:, i * size : (i + 1) * size], chunks[i], preferred_element_type=jnp.float32
        )
        total = part if total is None else total + part
    return total


def ask_kernel(lat_ref, wq_hbm, gain_ref, out_ref, wq, sem):
    fetches = start_chunks(wq_hbm, wq, sem)
    lat_norm = norm_rows(lat_ref[...].astype(jnp.float32), gain_ref[...]).astype(jnp.bfloat16)
    query = times_chunks(lat_norm, fetches, wq, None).astype(jnp.bfloat16)
    for j in range(out_ref.shape[0]):
        out_ref[j] = query


def ask(latents, w_query, gain, count):
    rows, width = latents.shape
    vmem = pl.BlockSpec(memory_space=pltpu.VMEM)
    return pl.pallas_call(
        ask_kernel,
        in_specs=[vmem, pl.BlockSpec(memory_space=pltpu.HBM), vmem],
        out_shape=jax.ShapeDtypeStruct((count, rows, width), jnp.bfloat16),
        scratch_shapes=[
            pltpu.VMEM((CHUNKS, width // CHUNKS, width), jnp.bfloat16),
            pltpu.SemaphoreType.DMA((CHUNKS,)),
        ],
        cost_estimate=pl.CostEstimate(
            flops=2 * rows * width * width,
            transcendentals=rows,
            bytes_accessed=2 * width * width + 2 * (count + 1) * rows * width,
        ),
        name="ask",
    )(latents, in_hbm(w_query), gain.reshape(1, width))


def mix_kernel(parts_ref, lat_ref, wo_hbm, gain_ref, res_ref, mlp_ref, wo, sem):
    rows, width = lat_ref.shape
    head_dim = width // HEADS
    fetches = start_chunks(wo_hbm, wo, sem)
    total = parts_ref[0].astype(jnp.float32)
    for j in range(1, parts_ref.shape[0]):
        total = total + parts_ref[j].astype(jnp.float32)
    denom = total[:, width : width + HEADS] + total[:, width + HEADS : width + 2 * HEADS]
    wide = jnp.concatenate(
        [jnp.broadcast_to(denom[:, h : h + 1], (rows, head_dim)) for h in range(HEADS)], axis=1
    )
    attended = (total[:, :width] / wide).astype(jnp.bfloat16)
    mixed = times_chunks(attended, fetches, wo, lat_ref[...].astype(jnp.float32))
    res_ref[...] = mixed.astype(jnp.bfloat16)
    mlp_in = norm_rows(mixed, gain_ref[...]).astype(jnp.bfloat16)
    for j in range(mlp_ref.shape[0]):
        mlp_ref[j] = mlp_in


def mix(parts, latents, w_out, gain):
    rows, width = latents.shape
    vmem = pl.BlockSpec(memory_space=pltpu.VMEM)
    return pl.pallas_call(
        mix_kernel,
        in_specs=[vmem, vmem, pl.BlockSpec(memory_space=pltpu.HBM), vmem],
        out_shape=[
            jax.ShapeDtypeStruct((rows, width), jnp.bfloat16),
            jax.ShapeDtypeStruct((parts.shape[0], rows, width), jnp.bfloat16),
        ],
        scratch_shapes=[
            pltpu.VMEM((CHUNKS, width // CHUNKS, width), jnp.bfloat16),
            pltpu.SemaphoreType.DMA((CHUNKS,)),
        ],
        cost_estimate=pl.CostEstimate(
            flops=2 * rows * width * width,
            transcendentals=rows,
            bytes_accessed=2 * width * width + 2 * parts.size,
        ),
        name="mix",
    )(parts, latents, in_hbm(w_out), gain.reshape(1, width))


def exchange(blocks):
    return lax.all_to_all(blocks, "page", 0, 0, tiled=True)


def spread_pairs(block, count):
    chips = count // 2
    sides = [[2 * chip + side for chip in range(chips)] for side in range(2)]
    everyone = jnp.broadcast_to(block[None], (chips,) + block.shape)
    mine = lax.all_to_all(everyone, "page", 0, 0, axis_index_groups=sides, tiled=True)
    theirs = lax.ppermute(mine, "page", [(i, i ^ 1) for i in range(count)])
    return mine, theirs


def body(
    latents,
    patches,
    lat_gain,
    patch_gain,
    mlp_gain,
    w_query,
    w_key,
    w_value,
    w_out,
    w_hidden,
    w_connect,
):
    count = lax.axis_size("page")
    lat_rows, width = latents.shape
    query = exchange(ask(latents, w_query, lat_gain, count)).reshape(count * lat_rows, width)
    keys, values = project(patches, patch_gain, w_key, w_value)
    packed = attend(query, keys, values)
    parts = exchange(packed.reshape(count, lat_rows, width + LANES))
    resampled, mlp_in = mix(parts, latents, w_out, mlp_gain)
    mlp_all = exchange(mlp_in).reshape(count * lat_rows, width)
    hidden = jax.nn.gelu(
        jnp.dot(mlp_all, w_hidden, preferred_element_type=jnp.float32), approximate=True
    ).astype(jnp.bfloat16)
    rows, units = hidden.shape
    mine, theirs = spread_pairs(hidden, count)
    even = lax.axis_index("page") % 2 == 0
    both = jnp.stack([jnp.where(even, mine, theirs), jnp.where(even, theirs, mine)], axis=1)
    hidden_all = jnp.transpose(both.reshape(count, rows, units), (1, 0, 2)).reshape(
        rows, count * units
    )
    connector = jnp.dot(hidden_all, w_connect, preferred_element_type=jnp.float32).astype(
        jnp.bfloat16
    )
    return (resampled, connector)


def solution(mesh):
    placed = (
        P(("slab", "page"), None),
        P(("slab", "page"), None),
        P(),
        P(),
        P(),
        P(),
        P(),
        P(),
        P(),
        P(None, "page"),
        P(None, "page"),
    )
    return jax.shard_map(
        body,
        mesh=mesh,
        in_specs=placed,
        out_specs=(P(("slab", "page"), None), P("slab", "page")),
        check_vma=False,
    )
```

```python
import math

import jax
import jax.numpy as jnp
from jax import lax
from jax.experimental import pallas as pl
from jax.experimental.pallas import tpu as pltpu
from jax.sharding import PartitionSpec as P

HEADS = 16
PACK = 4
LANES = 128
CHUNKS = 4
MIB = 1024 * 1024


def norm_rows(values_in, gain):
    center = values_in - jnp.mean(values_in, axis=-1, keepdims=True)
    spread = jnp.mean(center * center, axis=-1, keepdims=True)
    return center * lax.rsqrt(spread + 1e-05) * gain


def in_hbm(array):
    return pltpu.with_memory_space_constraint(array, pltpu.HBM)


def fixed(shape):
    return pl.BlockSpec(shape, lambda i: (0,) * len(shape), pipeline_mode=pl.Buffered(1))


def project_kernel(
    x_hbm, gain_ref, wk_hbm, wv_hbm, k_hbm, v_hbm, xs, wk, wv, ks, vs, pns, x_sem, w_sem, out_sem
):
    blocks, block, _ = xs.shape

    def fetch(i):
        return pltpu.make_async_copy(x_hbm.at[pl.ds(i * block, block)], xs.at[i], x_sem.at[i])

    def put(src, dst, which, i):
        return pltpu.make_async_copy(
            src.at[i], dst.at[pl.ds(i * block, block)], out_sem.at[which, i]
        )

    def normed(i):
        return norm_rows(xs[i].astype(jnp.float32), gain_ref[...]).astype(jnp.bfloat16)

    def times(weight, i):
        return jnp.dot(pns[i % 2], weight[...], preferred_element_type=jnp.float32).astype(
            jnp.bfloat16
        )

    key_copy = pltpu.make_async_copy(wk_hbm, wk, w_sem.at[0])
    value_copy = pltpu.make_async_copy(wv_hbm, wv, w_sem.at[1])
    fetch(0).start()
    key_copy.start()
    for i in range(1, min(2, blocks)):
        fetch(i).start()
    value_copy.start()
    for i in range(2, blocks):
        fetch(i).start()
    fetch(0).wait()
    pns[0] = normed(0)
    key_copy.wait()
    for i in range(blocks):
        ks[i] = times(wk, i)
        put(ks, k_hbm, 0, i).start()
        if i == 0:
            value_copy.wait()
        if i + 1 < blocks:
            fetch(i + 1).wait()
            pns[(i + 1) % 2] = normed(i + 1)
        vs[i] = times(wv, i)
        put(vs, v_hbm, 1, i).start()
    for i in range(blocks):
        put(ks, k_hbm, 0, i).wait()
        put(vs, v_hbm, 1, i).wait()


def project(patches, gain, w_key, w_value):
    rows, width = patches.shape
    block = math.gcd(rows, 512)
    blocks = rows // block
    hbm = pl.BlockSpec(memory_space=pltpu.HBM)
    return pl.pallas_call(
        project_kernel,
        in_specs=[hbm, pl.BlockSpec(memory_space=pltpu.VMEM), hbm, hbm],
        out_specs=[hbm, hbm],
        out_shape=[pltpu.HBM((rows, width), jnp.bfloat16)] * 2,
        scratch_shapes=[
            pltpu.VMEM((blocks, block, width), jnp.bfloat16),
            pltpu.VMEM((width, width), jnp.bfloat16),
            pltpu.VMEM((width, width), jnp.bfloat16),
            pltpu.VMEM((blocks, block, width), jnp.bfloat16),
            pltpu.VMEM((blocks, block, width), jnp.bfloat16),
            pltpu.VMEM((2, block, width), jnp.bfloat16),
            pltpu.SemaphoreType.DMA((blocks,)),
            pltpu.SemaphoreType.DMA((2,)),
            pltpu.SemaphoreType.DMA((2, blocks)),
        ],
        compiler_params=pltpu.CompilerParams(vmem_limit_bytes=32 * MIB),
        cost_estimate=pl.CostEstimate(
            flops=4 * rows * width * width,
            transcendentals=rows,
            bytes_accessed=6 * rows * width + 4 * width * width,
        ),
        name="project",
    )(in_hbm(patches), gain.reshape(1, width), in_hbm(w_key), in_hbm(w_value))


def attend_kernel(q_ref, k_ref, v_ref, out_ref, qbd, acc, dacc):
    step = pl.program_id(0)
    block = k_ref.shape[0]
    latents, width = q_ref.shape
    head_dim = width // HEADS
    span = PACK * head_dim
    groups = HEADS // PACK
    lane_head = lax.broadcasted_iota(jnp.int32, (latents, span), 1) // head_dim

    @pl.when(step == 0)
    def _():
        acc[...] = jnp.zeros_like(acc)
        dacc[...] = jnp.zeros_like(dacc)
        for g in range(groups):
            part = q_ref[:, g * span : (g + 1) * span]
            for h in range(PACK):
                qbd[g, h * latents : (h + 1) * latents, :] = jnp.where(
                    lane_head == h, part, jnp.zeros_like(part)
                )

    factor = math.log2(math.e) / math.sqrt(head_dim)
    for g in range(groups):
        cols = slice(g * span, (g + 1) * span)
        scores = lax.dot_general(
            qbd[g], k_ref[:, cols], (((1,), (1,)), ((), ())), preferred_element_type=jnp.float32
        )
        expo = jnp.exp2(scores * factor)
        total = expo[:, :LANES]
        for j in range(1, block // LANES):
            total = total + expo[:, j * LANES : (j + 1) * LANES]
        dacc[g] += total
        acc[g] += jnp.dot(
            expo.astype(jnp.bfloat16), v_ref[:, cols], preferred_element_type=jnp.float32
        )

    @pl.when(step == pl.num_programs(0) - 1)
    def _():
        lane = lax.broadcasted_iota(jnp.int32, (latents, LANES), 1)
        out = jnp.zeros((latents, LANES), jnp.float32)
        for g in range(groups):
            sums = jnp.sum(dacc[g], axis=-1, keepdims=True)
            high = sums.astype(jnp.bfloat16).astype(jnp.float32)
            low = sums - high
            picked = jnp.zeros((latents, span), jnp.float32)
            for h in range(PACK):
                rows = slice(h * latents, (h + 1) * latents)
                picked = jnp.where(lane_head == h, acc[g, rows, :], picked)
                out = jnp.where(lane == g * PACK + h, high[rows], out)
                out = jnp.where(lane == HEADS + g * PACK + h, low[rows], out)
            out_ref[:, g * span : (g + 1) * span] = picked.astype(jnp.bfloat16)
        out_ref[:, width:] = out.astype(jnp.bfloat16)


def attend(query, keys, values):
    rows, width = keys.shape
    count = query.shape[0]
    block = math.gcd(rows, 512)
    span = PACK * (width // HEADS)
    groups = HEADS // PACK
    tile = pl.BlockSpec((block, width), lambda i: (i, 0))
    return pl.pallas_call(
        attend_kernel,
        grid=(rows // block,),
        in_specs=[fixed((count, width)), tile, tile],
        out_specs=pl.BlockSpec((count, width + LANES), lambda i: (0, 0)),
        out_shape=jax.ShapeDtypeStruct((count, width + LANES), jnp.bfloat16),
        scratch_shapes=[
            pltpu.VMEM((groups, PACK * count, span), jnp.bfloat16),
            pltpu.VMEM((groups, PACK * count, span), jnp.float32),
            pltpu.VMEM((groups, PACK * count, LANES), jnp.float32),
        ],
        compiler_params=pltpu.CompilerParams(
            dimension_semantics=("arbitrary",), vmem_limit_bytes=30 * MIB
        ),
        cost_estimate=pl.CostEstimate(
            flops=4 * rows * count * PACK * width,
            transcendentals=rows * count * HEADS,
            bytes_accessed=4 * rows * width,
        ),
        name="attend",
    )(query, in_hbm(keys), in_hbm(values))


def start_chunks(hbm, chunks, sem):
    size = chunks.shape[1]
    fetches = [
        pltpu.make_async_copy(hbm.at[pl.ds(i * size, size)], chunks.at[i], sem.at[i])
        for i in range(chunks.shape[0])
    ]
    for fetch in fetches:
        fetch.start()
    return fetches


def times_chunks(rows, fetches, chunks, total):
    size = chunks.shape[1]
    for i, fetch in enumerate(fetches):
        fetch.wait()
        part = jnp.dot(
            rows[:, i * size : (i + 1) * size], chunks[i], preferred_element_type=jnp.float32
        )
        total = part if total is None else total + part
    return total


def ask_kernel(lat_ref, wq_hbm, gain_ref, out_ref, wq, sem):
    fetches = start_chunks(wq_hbm, wq, sem)
    lat_norm = norm_rows(lat_ref[...].astype(jnp.float32), gain_ref[...]).astype(jnp.bfloat16)
    query = times_chunks(lat_norm, fetches, wq, None).astype(jnp.bfloat16)
    for j in range(out_ref.shape[0]):
        out_ref[j] = query


def ask(latents, w_query, gain, count):
    rows, width = latents.shape
    vmem = pl.BlockSpec(memory_space=pltpu.VMEM)
    return pl.pallas_call(
        ask_kernel,
        in_specs=[vmem, pl.BlockSpec(memory_space=pltpu.HBM), vmem],
        out_shape=jax.ShapeDtypeStruct((count, rows, width), jnp.bfloat16),
        scratch_shapes=[
            pltpu.VMEM((CHUNKS, width // CHUNKS, width), jnp.bfloat16),
            pltpu.SemaphoreType.DMA((CHUNKS,)),
        ],
        cost_estimate=pl.CostEstimate(
            flops=2 * rows * width * width,
            transcendentals=rows,
            bytes_accessed=2 * width * width + 2 * (count + 1) * rows * width,
        ),
        name="ask",
    )(latents, in_hbm(w_query), gain.reshape(1, width))


def exchange(blocks):
    return lax.all_to_all(blocks, "page", 0, 0, tiled=True)


def spread(block, count):
    return jnp.broadcast_to(block[None], (count,) + block.shape)


def exchange_side(blocks, count):
    sides = [[2 * chip + side for chip in range(count // 2)] for side in range(2)]
    return lax.all_to_all(blocks, "page", 0, 0, axis_index_groups=sides, tiled=True)


def join_sides(mine, count):
    theirs = lax.ppermute(mine, "page", [(i, i ^ 1) for i in range(count)])
    even = lax.axis_index("page") % 2 == 0
    both = jnp.stack([jnp.where(even, mine, theirs), jnp.where(even, theirs, mine)], axis=1)
    return both.reshape((count,) + mine.shape[1:])


def body(
    latents,
    patches,
    lat_gain,
    patch_gain,
    mlp_gain,
    w_query,
    w_key,
    w_value,
    w_out,
    w_hidden,
    w_connect,
):
    count = lax.axis_size("page")
    lat_rows, width = latents.shape
    query_side = exchange_side(ask(latents, w_query, lat_gain, count // 2), count)
    keys, values = project(patches, patch_gain, w_key, w_value)
    query_side, keys, values = lax.optimization_barrier((query_side, keys, values))
    query = join_sides(query_side, count).reshape(count * lat_rows, width)
    packed = attend(query, keys, values)
    parts = exchange(packed.reshape(count, lat_rows, width + LANES))
    summed = jnp.sum(parts.astype(jnp.float32), axis=0)
    denom = summed[:, width : width + HEADS] + summed[:, width + HEADS : width + 2 * HEADS]
    attended = (
        (summed[:, :width].reshape(lat_rows, HEADS, width // HEADS) / denom[:, :, None])
        .reshape(lat_rows, width)
        .astype(jnp.bfloat16)
    )
    mixed = latents.astype(jnp.float32) + jnp.dot(
        attended, w_out, preferred_element_type=jnp.float32
    )
    resampled = mixed.astype(jnp.bfloat16)
    mlp_in = norm_rows(mixed, mlp_gain).astype(jnp.bfloat16)
    mlp_all = exchange(spread(mlp_in, count)).reshape(count * lat_rows, width)
    hidden = jax.nn.gelu(
        jnp.dot(mlp_all, w_hidden, preferred_element_type=jnp.float32), approximate=True
    ).astype(jnp.bfloat16)
    rows, units = hidden.shape
    hidden_all = join_sides(exchange_side(spread(hidden, count // 2), count), count)
    hidden_all = jnp.transpose(hidden_all, (1, 0, 2)).reshape(rows, count * units)
    connector = jnp.dot(hidden_all, w_connect, preferred_element_type=jnp.float32).astype(
        jnp.bfloat16
    )
    return (resampled, connector)


def solution(mesh):
    placed = (
        P(("slab", "page"), None),
        P(("slab", "page"), None),
        P(),
        P(),
        P(),
        P(),
        P(),
        P(),
        P(),
        P(None, "page"),
        P(None, "page"),
    )
    return jax.shard_map(
        body,
        mesh=mesh,
        in_specs=placed,
        out_specs=(P(("slab", "page"), None), P("slab", "page")),
        check_vma=False,
    )
```

```python
import math

import jax
import jax.numpy as jnp
from jax import lax
from jax.experimental import pallas as pl
from jax.experimental.pallas import tpu as pltpu
from jax.sharding import PartitionSpec as P

HEADS = 16
PACK = 4
LANES = 128
BLOCK = 512
MIB = 1024 * 1024


def norm_rows(values_in, gain):
    center = values_in - jnp.mean(values_in, axis=-1, keepdims=True)
    spread = jnp.mean(center * center, axis=-1, keepdims=True)
    return center * lax.rsqrt(spread + 1e-05) * gain


def in_hbm(array):
    return pltpu.with_memory_space_constraint(array, pltpu.HBM)


def project_rows(get, gain_ref, wk, wv, ks, vs, pns, waits, base, keys_ready=None):
    blocks = len(waits)
    block = pns.shape[1]

    def normed(i):
        return norm_rows(get(i).astype(jnp.float32), gain_ref[...]).astype(jnp.bfloat16)

    def times(weight, i):
        return jnp.dot(pns[i % 2], weight[...], preferred_element_type=jnp.float32).astype(
            jnp.bfloat16
        )

    waits[0][0].wait()
    pns[0] = normed(0)
    for i in range(blocks):
        rows = pl.ds(base + i * block, block)
        if i == 0:
            waits[0][1].wait()
        ks[rows, :] = times(wk, i)
        if keys_ready is not None:
            keys_ready()
        if i == 0:
            waits[0][2].wait()
        if i + 1 < blocks:
            waits[i + 1][0].wait()
            pns[(i + 1) % 2] = normed(i + 1)
        vs[rows, :] = times(wv, i)


def early_kernel(
    x_hbm, gain_hbm, wk_hbm, wv_hbm, k_hbm, v_hbm, gain_ref, xs, wk, wv, ks, vs, pns, sem
):
    gain_copy = pltpu.make_async_copy(gain_hbm, gain_ref, sem.at[3])
    fetches = [
        pltpu.make_async_copy(x_hbm.at[pl.ds(0, xs.shape[0])], xs, sem.at[0]),
        pltpu.make_async_copy(wk_hbm, wk, sem.at[1]),
        pltpu.make_async_copy(wv_hbm, wv, sem.at[2]),
    ]
    gain_copy.start()
    for fetch in fetches:
        fetch.start()
    key_put = pltpu.make_async_copy(ks, k_hbm, sem.at[4])
    value_put = pltpu.make_async_copy(vs, v_hbm, sem.at[5])
    gain_copy.wait()
    project_rows(
        lambda i: xs[...], gain_ref, wk, wv, ks, vs, pns, [fetches], 0, key_put.start
    )
    value_put.start()
    key_put.wait()
    value_put.wait()


def early(patches, gain, w_key, w_value, block):
    width = patches.shape[1]
    hbm = pl.BlockSpec(memory_space=pltpu.HBM)
    return pl.pallas_call(
        early_kernel,
        in_specs=[hbm] * 4,
        out_specs=[hbm] * 2,
        out_shape=[pltpu.HBM((block, width), jnp.bfloat16)] * 2,
        scratch_shapes=[
            pltpu.VMEM((1, width), jnp.float32),
            pltpu.VMEM((block, width), jnp.bfloat16),
            pltpu.VMEM((width, width), jnp.bfloat16),
            pltpu.VMEM((width, width), jnp.bfloat16),
            pltpu.VMEM((block, width), jnp.bfloat16),
            pltpu.VMEM((block, width), jnp.bfloat16),
            pltpu.VMEM((1, block, width), jnp.bfloat16),
            pltpu.SemaphoreType.DMA((6,)),
        ],
        compiler_params=pltpu.CompilerParams(vmem_limit_bytes=24 * MIB),
        cost_estimate=pl.CostEstimate(
            flops=4 * block * width * width,
            transcendentals=block,
            bytes_accessed=6 * block * width + 4 * width * width,
        ),
        name="early",
    )(in_hbm(patches), in_hbm(gain.reshape(1, width)), in_hbm(w_key), in_hbm(w_value))


def attend_kernel(
    lat_ref,
    lat_gain_ref,
    wq_hbm,
    x_hbm,
    gain_hbm,
    wk_hbm,
    wv_hbm,
    k_hbm,
    v_hbm,
    out_ref,
    gain_ref,
    xs,
    wk,
    wv,
    wq,
    ks,
    vs,
    pns,
    x_sem,
    w_sem,
):
    latents, width = lat_ref.shape
    blocks, block, _ = xs.shape
    rows = ks.shape[0]
    head_dim = width // HEADS
    span = PACK * head_dim
    groups = HEADS // PACK
    fetches = [
        pltpu.make_async_copy(x_hbm.at[pl.ds((i + 1) * block, block)], xs.at[i], x_sem.at[i])
        for i in range(blocks)
    ]
    key_copy = pltpu.make_async_copy(wk_hbm, wk, w_sem.at[0])
    value_copy = pltpu.make_async_copy(wv_hbm, wv, w_sem.at[1])
    later = [
        pltpu.make_async_copy(wq_hbm, wq, w_sem.at[2]),
        pltpu.make_async_copy(k_hbm, ks.at[pl.ds(0, block)], w_sem.at[3]),
        pltpu.make_async_copy(v_hbm, vs.at[pl.ds(0, block)], w_sem.at[4]),
    ]
    gain_copy = pltpu.make_async_copy(gain_hbm, gain_ref, w_sem.at[5])
    gain_copy.start()
    fetches[0].start()
    key_copy.start()
    value_copy.start()
    for fetch in fetches[1:] + later:
        fetch.start()
    lat_norm = norm_rows(lat_ref[...].astype(jnp.float32), lat_gain_ref[...]).astype(jnp.bfloat16)
    gain_copy.wait()
    waits = [(fetches[0], key_copy, value_copy)] + [(fetch,) for fetch in fetches[1:]]
    project_rows(lambda i: xs[i], gain_ref, wk, wv, ks, vs, pns, waits, block)
    for fetch in later:
        fetch.wait()
    query = jnp.dot(lat_norm, wq[...], preferred_element_type=jnp.float32).astype(jnp.bfloat16)

    lane_head = lax.broadcasted_iota(jnp.int32, (latents, span), 1) // head_dim
    lane = lax.broadcasted_iota(jnp.int32, (latents, LANES), 1)
    factor = math.log2(math.e) / math.sqrt(head_dim)
    piece = rows if PACK * latents <= 512 else block
    out = jnp.zeros((latents, LANES), jnp.float32)
    for g in range(groups):
        cols = slice(g * span, (g + 1) * span)
        part = query[:, cols]
        apart = jnp.concatenate(
            [jnp.where(lane_head == h, part, jnp.zeros_like(part)) for h in range(PACK)], axis=0
        )
        total = numer = None
        for start in range(0, rows, piece):
            scores = lax.dot_general(
                apart,
                ks[start : start + piece, cols],
                (((1,), (1,)), ((), ())),
                preferred_element_type=jnp.float32,
            )
            expo = jnp.exp2(scores * factor)
            for j in range(piece // LANES):
                lanes = expo[:, j * LANES : (j + 1) * LANES]
                total = lanes if total is None else total + lanes
            here = jnp.dot(
                expo.astype(jnp.bfloat16),
                vs[start : start + piece, cols],
                preferred_element_type=jnp.float32,
            )
            numer = here if numer is None else numer + here
        sums = jnp.sum(total, axis=-1, keepdims=True)
        high = sums.astype(jnp.bfloat16).astype(jnp.float32)
        low = sums - high
        picked = jnp.zeros((latents, span), jnp.float32)
        for h in range(PACK):
            mine = slice(h * latents, (h + 1) * latents)
            picked = jnp.where(lane_head == h, numer[mine], picked)
            out = jnp.where(lane == g * PACK + h, high[mine], out)
            out = jnp.where(lane == HEADS + g * PACK + h, low[mine], out)
        out_ref[:, cols] = picked.astype(jnp.bfloat16)
    out_ref[:, width:] = out.astype(jnp.bfloat16)


def attend(latents, lat_gain, w_query, patches, gain, w_key, w_value, keys, values):
    rows, width = patches.shape
    block = keys.shape[0]
    blocks = rows // block - 1
    count = latents.shape[0]
    vmem = pl.BlockSpec(memory_space=pltpu.VMEM)
    hbm = pl.BlockSpec(memory_space=pltpu.HBM)
    return pl.pallas_call(
        attend_kernel,
        in_specs=[vmem, vmem] + [hbm] * 7,
        out_specs=vmem,
        out_shape=jax.ShapeDtypeStruct((count, width + LANES), jnp.bfloat16),
        scratch_shapes=[
            pltpu.VMEM((1, width), jnp.float32),
            pltpu.VMEM((blocks, block, width), jnp.bfloat16),
            pltpu.VMEM((width, width), jnp.bfloat16),
            pltpu.VMEM((width, width), jnp.bfloat16),
            pltpu.VMEM((width, width), jnp.bfloat16),
            pltpu.VMEM((rows, width), jnp.bfloat16),
            pltpu.VMEM((rows, width), jnp.bfloat16),
            pltpu.VMEM((2, block, width), jnp.bfloat16),
            pltpu.SemaphoreType.DMA((blocks,)),
            pltpu.SemaphoreType.DMA((6,)),
        ],
        compiler_params=pltpu.CompilerParams(vmem_limit_bytes=42 * MIB),
        cost_estimate=pl.CostEstimate(
            flops=4 * (rows - block) * width * width + 4 * rows * count * PACK * width,
            transcendentals=rows * count * HEADS,
            bytes_accessed=2 * rows * width + 6 * width * width,
        ),
        name="attend",
    )(
        latents,
        lat_gain.reshape(1, width),
        in_hbm(w_query),
        in_hbm(patches),
        in_hbm(gain.reshape(1, width)),
        in_hbm(w_key),
        in_hbm(w_value),
        in_hbm(keys),
        in_hbm(values),
    )


def exchange(blocks):
    return lax.all_to_all(blocks, "page", 0, 0, tiled=True)


def spread(block, count):
    return jnp.broadcast_to(block[None], (count,) + block.shape)


def exchange_side(blocks, count):
    sides = [[2 * chip + side for chip in range(count // 2)] for side in range(2)]
    return lax.all_to_all(blocks, "page", 0, 0, axis_index_groups=sides, tiled=True)


def join_sides(mine, count):
    theirs = lax.ppermute(mine, "page", [(i, i ^ 1) for i in range(count)])
    even = lax.axis_index("page") % 2 == 0
    both = jnp.stack([jnp.where(even, mine, theirs), jnp.where(even, theirs, mine)], axis=1)
    return both.reshape((count,) + mine.shape[1:])


def body(
    latents,
    patches,
    lat_gain,
    patch_gain,
    mlp_gain,
    w_query,
    w_key,
    w_value,
    w_out,
    w_hidden,
    w_connect,
):
    count = lax.axis_size("page")
    lat_rows, width = latents.shape
    lat_all = exchange(spread(latents, count)).reshape(count * lat_rows, width)
    block = math.gcd(patches.shape[0], BLOCK)
    keys, values = early(patches, patch_gain, w_key, w_value, block)
    packed = attend(
        lat_all, lat_gain, w_query, patches, patch_gain, w_key, w_value, keys, values
    )
    parts = exchange(packed.reshape(count, lat_rows, width + LANES))
    summed = jnp.sum(parts.astype(jnp.float32), axis=0)
    denom = summed[:, width : width + HEADS] + summed[:, width + HEADS : width + 2 * HEADS]
    attended = (
        (summed[:, :width].reshape(lat_rows, HEADS, width // HEADS) / denom[:, :, None])
        .reshape(lat_rows, width)
        .astype(jnp.bfloat16)
    )
    mixed = latents.astype(jnp.float32) + jnp.dot(
        attended, w_out, preferred_element_type=jnp.float32
    )
    resampled = mixed.astype(jnp.bfloat16)
    mlp_in = norm_rows(mixed, mlp_gain).astype(jnp.bfloat16)
    mlp_all = exchange(spread(mlp_in, count)).reshape(count * lat_rows, width)
    hidden = jax.nn.gelu(
        jnp.dot(mlp_all, w_hidden, preferred_element_type=jnp.float32), approximate=True
    ).astype(jnp.bfloat16)
    rows, units = hidden.shape
    hidden_all = join_sides(exchange_side(spread(hidden, count // 2), count), count)
    hidden_all = jnp.transpose(hidden_all, (1, 0, 2)).reshape(rows, count * units)
    connector = jnp.dot(hidden_all, w_connect, preferred_element_type=jnp.float32).astype(
        jnp.bfloat16
    )
    return (resampled, connector)


def solution(mesh):
    placed = (
        P(("slab", "page"), None),
        P(("slab", "page"), None),
        P(),
        P(),
        P(),
        P(),
        P(),
        P(),
        P(),
        P(None, "page"),
        P(None, "page"),
    )
    return jax.shard_map(
        body,
        mesh=mesh,
        in_specs=placed,
        out_specs=(P(("slab", "page"), None), P("slab", "page")),
        check_vma=False,
    )
```

```python
import math

import jax
import jax.numpy as jnp
from jax import lax
from jax.experimental import pallas as pl
from jax.experimental.pallas import tpu as pltpu
from jax.sharding import PartitionSpec as P

HEADS = 16
PACK = 4
LANES = 128
BLOCK = 512
CHUNKS = 4
MIB = 1024 * 1024


def norm_rows(values_in, gain):
    center = values_in - jnp.mean(values_in, axis=-1, keepdims=True)
    spread = jnp.mean(center * center, axis=-1, keepdims=True)
    return center * lax.rsqrt(spread + 1e-05) * gain


def in_hbm(array):
    return pltpu.with_memory_space_constraint(array, pltpu.HBM)


def project_rows(get, gain_ref, wk, wv, ks, vs, pns, waits, base, keys_ready=None):
    blocks = len(waits)
    block = pns.shape[1]

    def normed(i):
        return norm_rows(get(i).astype(jnp.float32), gain_ref[...]).astype(jnp.bfloat16)

    def times(weight, i):
        return jnp.dot(pns[i % 2], weight[...], preferred_element_type=jnp.float32).astype(
            jnp.bfloat16
        )

    waits[0][0].wait()
    pns[0] = normed(0)
    for i in range(blocks):
        rows = pl.ds(base + i * block, block)
        if i == 0:
            size = ks.shape[1] // len(waits[0][1])
            for j, fetch in enumerate(waits[0][1]):
                cols = pl.ds(j * size, size)
                fetch.wait()
                ks[rows, cols] = jnp.dot(
                    pns[0], wk[:, cols], preferred_element_type=jnp.float32
                ).astype(jnp.bfloat16)
        else:
            ks[rows, :] = times(wk, i)
        if keys_ready is not None:
            keys_ready()
        if i == 0:
            waits[0][2].wait()
        if i + 1 < blocks:
            waits[i + 1][0].wait()
            pns[(i + 1) % 2] = normed(i + 1)
        vs[rows, :] = times(wv, i)


def column_copies(hbm, ref, sem):
    size = ref.shape[1] // CHUNKS
    return [
        pltpu.make_async_copy(
            hbm.at[:, pl.ds(j * size, size)], ref.at[:, pl.ds(j * size, size)], sem.at[j]
        )
        for j in range(CHUNKS)
    ]


def early_kernel(
    x_hbm, gain_hbm, wk_hbm, wv_hbm, k_hbm, v_hbm, gain_ref, xs, wk, wv, ks, vs, pns, sem, wk_sem
):
    gain_copy = pltpu.make_async_copy(gain_hbm, gain_ref, sem.at[2])
    x_copy = pltpu.make_async_copy(x_hbm.at[pl.ds(0, xs.shape[0])], xs, sem.at[0])
    key_copies = column_copies(wk_hbm, wk, wk_sem)
    value_copy = pltpu.make_async_copy(wv_hbm, wv, sem.at[1])
    fetches = (x_copy, key_copies, value_copy)
    gain_copy.start()
    for fetch in [x_copy] + key_copies + [value_copy]:
        fetch.start()
    key_put = pltpu.make_async_copy(ks, k_hbm, sem.at[3])
    value_put = pltpu.make_async_copy(vs, v_hbm, sem.at[4])
    gain_copy.wait()
    project_rows(
        lambda i: xs[...], gain_ref, wk, wv, ks, vs, pns, [fetches], 0, key_put.start
    )
    value_put.start()
    key_put.wait()
    value_put.wait()


def early(patches, gain, w_key, w_value, block):
    width = patches.shape[1]
    hbm = pl.BlockSpec(memory_space=pltpu.HBM)
    return pl.pallas_call(
        early_kernel,
        in_specs=[hbm] * 4,
        out_specs=[hbm] * 2,
        out_shape=[pltpu.HBM((block, width), jnp.bfloat16)] * 2,
        scratch_shapes=[
            pltpu.VMEM((1, width), jnp.float32),
            pltpu.VMEM((block, width), jnp.bfloat16),
            pltpu.VMEM((width, width), jnp.bfloat16),
            pltpu.VMEM((width, width), jnp.bfloat16),
            pltpu.VMEM((block, width), jnp.bfloat16),
            pltpu.VMEM((block, width), jnp.bfloat16),
            pltpu.VMEM((1, block, width), jnp.bfloat16),
            pltpu.SemaphoreType.DMA((5,)),
            pltpu.SemaphoreType.DMA((CHUNKS,)),
        ],
        compiler_params=pltpu.CompilerParams(vmem_limit_bytes=24 * MIB),
        cost_estimate=pl.CostEstimate(
            flops=4 * block * width * width,
            transcendentals=block,
            bytes_accessed=6 * block * width + 4 * width * width,
        ),
        name="early",
    )(in_hbm(patches), in_hbm(gain.reshape(1, width)), in_hbm(w_key), in_hbm(w_value))


def attend_kernel(
    lat_ref,
    lat_gain_ref,
    wq_hbm,
    x_hbm,
    gain_hbm,
    wk_hbm,
    wv_hbm,
    k_hbm,
    v_hbm,
    out_ref,
    gain_ref,
    xs,
    wk,
    wv,
    wq,
    ks,
    vs,
    pns,
    x_sem,
    w_sem,
    wk_sem,
):
    latents, width = lat_ref.shape
    blocks, block, _ = xs.shape
    rows = ks.shape[0]
    head_dim = width // HEADS
    span = PACK * head_dim
    groups = HEADS // PACK
    fetches = [
        pltpu.make_async_copy(x_hbm.at[pl.ds((i + 1) * block, block)], xs.at[i], x_sem.at[i])
        for i in range(blocks)
    ]
    key_copies = column_copies(wk_hbm, wk, wk_sem)
    value_copy = pltpu.make_async_copy(wv_hbm, wv, w_sem.at[0])
    later = [
        pltpu.make_async_copy(wq_hbm, wq, w_sem.at[1]),
        pltpu.make_async_copy(k_hbm, ks.at[pl.ds(0, block)], w_sem.at[2]),
        pltpu.make_async_copy(v_hbm, vs.at[pl.ds(0, block)], w_sem.at[3]),
    ]
    gain_copy = pltpu.make_async_copy(gain_hbm, gain_ref, w_sem.at[4])
    gain_copy.start()
    fetches[0].start()
    for fetch in key_copies:
        fetch.start()
    value_copy.start()
    for fetch in fetches[1:] + later:
        fetch.start()
    lat_norm = norm_rows(lat_ref[...].astype(jnp.float32), lat_gain_ref[...]).astype(jnp.bfloat16)
    gain_copy.wait()
    waits = [(fetches[0], key_copies, value_copy)] + [(fetch,) for fetch in fetches[1:]]
    project_rows(lambda i: xs[i], gain_ref, wk, wv, ks, vs, pns, waits, block)
    for fetch in later:
        fetch.wait()
    query = jnp.dot(lat_norm, wq[...], preferred_element_type=jnp.float32).astype(jnp.bfloat16)

    lane_head = lax.broadcasted_iota(jnp.int32, (latents, span), 1) // head_dim
    lane = lax.broadcasted_iota(jnp.int32, (latents, LANES), 1)
    factor = math.log2(math.e) / math.sqrt(head_dim)
    piece = rows if PACK * latents <= 512 else block
    out = jnp.zeros((latents, LANES), jnp.float32)
    for g in range(groups):
        cols = slice(g * span, (g + 1) * span)
        part = query[:, cols]
        apart = jnp.concatenate(
            [jnp.where(lane_head == h, part, jnp.zeros_like(part)) for h in range(PACK)], axis=0
        )
        total = numer = None
        for start in range(0, rows, piece):
            scores = lax.dot_general(
                apart,
                ks[start : start + piece, cols],
                (((1,), (1,)), ((), ())),
                preferred_element_type=jnp.float32,
            )
            expo = jnp.exp2(scores * factor)
            for j in range(piece // LANES):
                lanes = expo[:, j * LANES : (j + 1) * LANES]
                total = lanes if total is None else total + lanes
            here = jnp.dot(
                expo.astype(jnp.bfloat16),
                vs[start : start + piece, cols],
                preferred_element_type=jnp.float32,
            )
            numer = here if numer is None else numer + here
        sums = jnp.sum(total, axis=-1, keepdims=True)
        high = sums.astype(jnp.bfloat16).astype(jnp.float32)
        low = sums - high
        picked = jnp.zeros((latents, span), jnp.float32)
        for h in range(PACK):
            mine = slice(h * latents, (h + 1) * latents)
            picked = jnp.where(lane_head == h, numer[mine], picked)
            out = jnp.where(lane == g * PACK + h, high[mine], out)
            out = jnp.where(lane == HEADS + g * PACK + h, low[mine], out)
        out_ref[:, cols] = picked.astype(jnp.bfloat16)
    out_ref[:, width:] = out.astype(jnp.bfloat16)


def attend(latents, lat_gain, w_query, patches, gain, w_key, w_value, keys, values):
    rows, width = patches.shape
    block = keys.shape[0]
    blocks = rows // block - 1
    count = latents.shape[0]
    vmem = pl.BlockSpec(memory_space=pltpu.VMEM)
    hbm = pl.BlockSpec(memory_space=pltpu.HBM)
    return pl.pallas_call(
        attend_kernel,
        in_specs=[vmem, vmem] + [hbm] * 7,
        out_specs=vmem,
        out_shape=jax.ShapeDtypeStruct((count, width + LANES), jnp.bfloat16),
        scratch_shapes=[
            pltpu.VMEM((1, width), jnp.float32),
            pltpu.VMEM((blocks, block, width), jnp.bfloat16),
            pltpu.VMEM((width, width), jnp.bfloat16),
            pltpu.VMEM((width, width), jnp.bfloat16),
            pltpu.VMEM((width, width), jnp.bfloat16),
            pltpu.VMEM((rows, width), jnp.bfloat16),
            pltpu.VMEM((rows, width), jnp.bfloat16),
            pltpu.VMEM((2, block, width), jnp.bfloat16),
            pltpu.SemaphoreType.DMA((blocks,)),
            pltpu.SemaphoreType.DMA((5,)),
            pltpu.SemaphoreType.DMA((CHUNKS,)),
        ],
        compiler_params=pltpu.CompilerParams(vmem_limit_bytes=42 * MIB),
        cost_estimate=pl.CostEstimate(
            flops=4 * (rows - block) * width * width + 4 * rows * count * PACK * width,
            transcendentals=rows * count * HEADS,
            bytes_accessed=2 * rows * width + 6 * width * width,
        ),
        name="attend",
    )(
        latents,
        lat_gain.reshape(1, width),
        in_hbm(w_query),
        in_hbm(patches),
        in_hbm(gain.reshape(1, width)),
        in_hbm(w_key),
        in_hbm(w_value),
        in_hbm(keys),
        in_hbm(values),
    )


def copies_kernel(x_hbm, out_hbm, sem):
    puts = [
        pltpu.make_async_copy(x_hbm, out_hbm.at[j], sem.at[j]) for j in range(out_hbm.shape[0])
    ]
    for put in puts:
        put.start()
    for put in puts:
        put.wait()


def copies(block, count):
    hbm = pl.BlockSpec(memory_space=pltpu.HBM)
    return pl.pallas_call(
        copies_kernel,
        in_specs=[hbm],
        out_specs=hbm,
        out_shape=jax.ShapeDtypeStruct((count,) + block.shape, block.dtype),
        scratch_shapes=[pltpu.SemaphoreType.DMA((count,))],
        compiler_params=pltpu.CompilerParams(vmem_limit_bytes=MIB),
        name="copies",
    )(in_hbm(block))


def exchange(blocks):
    return lax.all_to_all(blocks, "page", 0, 0, tiled=True)


def spread(block, count):
    return jnp.broadcast_to(block[None], (count,) + block.shape)


def exchange_side(blocks, count):
    sides = [[2 * chip + side for chip in range(count // 2)] for side in range(2)]
    return lax.all_to_all(blocks, "page", 0, 0, axis_index_groups=sides, tiled=True)


def swap_cores(array, count):
    return lax.ppermute(array, "page", [(i, i ^ 1) for i in range(count)])


def by_side(even, mine, theirs, axis):
    return jnp.concatenate([jnp.where(even, mine, theirs), jnp.where(even, theirs, mine)], axis=axis)


def body(
    latents,
    patches,
    lat_gain,
    patch_gain,
    mlp_gain,
    w_query,
    w_key,
    w_value,
    w_out,
    w_hidden,
    w_connect,
):
    count = lax.axis_size("page")
    lat_rows, width = latents.shape
    lat_all = exchange(copies(latents, count)).reshape(count * lat_rows, width)
    block = math.gcd(patches.shape[0], BLOCK)
    keys, values = early(patches, patch_gain, w_key, w_value, block)
    even = lax.axis_index("page") % 2 == 0
    lat_all, w_theirs, even = lax.optimization_barrier(
        (lat_all, swap_cores(w_hidden, count), even)
    )
    packed = attend(
        lat_all, lat_gain, w_query, patches, patch_gain, w_key, w_value, keys, values
    )
    parts = exchange(packed.reshape(count, lat_rows, width + LANES))
    summed = jnp.sum(parts.astype(jnp.float32), axis=0)
    denom = summed[:, width : width + HEADS] + summed[:, width + HEADS : width + 2 * HEADS]
    attended = (
        (summed[:, :width].reshape(lat_rows, HEADS, width // HEADS) / denom[:, :, None])
        .reshape(lat_rows, width)
        .astype(jnp.bfloat16)
    )
    mixed = latents.astype(jnp.float32) + jnp.dot(
        attended, w_out, preferred_element_type=jnp.float32
    )
    resampled = mixed.astype(jnp.bfloat16)
    mlp_in = norm_rows(mixed, mlp_gain).astype(jnp.bfloat16)
    chips = count // 2
    rows = chips * lat_rows
    mlp_side = exchange_side(spread(mlp_in, chips), count).reshape(rows, width)

    def hidden_of(weight):
        return jax.nn.gelu(
            jnp.dot(mlp_side, weight, preferred_element_type=jnp.float32), approximate=True
        ).astype(jnp.bfloat16)

    hidden = by_side(even, hidden_of(w_hidden), hidden_of(w_theirs), 1)
    hidden_mine = exchange_side(spread(hidden, chips), count)
    hidden_theirs = swap_cores(hidden_mine, count)

    def connect(blocks):
        flat = jnp.transpose(blocks, (1, 0, 2)).reshape(rows, w_connect.shape[0])
        return jnp.dot(flat, w_connect, preferred_element_type=jnp.float32).astype(jnp.bfloat16)

    sides = [
        part.reshape(chips, 1, lat_rows, w_connect.shape[1])
        for part in (connect(hidden_mine), connect(hidden_theirs))
    ]
    connector = by_side(even, sides[0], sides[1], 1).reshape(count * lat_rows, w_connect.shape[1])
    return (resampled, connector)


def solution(mesh):
    placed = (
        P(("slab", "page"), None),
        P(("slab", "page"), None),
        P(),
        P(),
        P(),
        P(),
        P(),
        P(),
        P(),
        P(None, "page"),
        P(None, "page"),
    )
    return jax.shard_map(
        body,
        mesh=mesh,
        in_specs=placed,
        out_specs=(P(("slab", "page"), None), P("slab", "page")),
        check_vma=False,
    )
```

```python
import math

import jax
import jax.numpy as jnp
from jax import lax
from jax.experimental import pallas as pl
from jax.experimental.pallas import tpu as pltpu
from jax.sharding import PartitionSpec as P

HEADS = 16
PACK = 4
LANES = 128
BLOCK = 512
MIB = 1024 * 1024


def norm_rows(values_in, gain):
    center = values_in - jnp.mean(values_in, axis=-1, keepdims=True)
    spread = jnp.mean(center * center, axis=-1, keepdims=True)
    return center * lax.rsqrt(spread + 1e-05) * gain


def in_hbm(array):
    return pltpu.with_memory_space_constraint(array, pltpu.HBM)


def project_rows(get, gain_ref, wk, wv, ks, vs, pns, waits, base, keys_ready=None):
    blocks = len(waits)
    block = pns.shape[1]

    def normed(i):
        return norm_rows(get(i).astype(jnp.float32), gain_ref[...]).astype(jnp.bfloat16)

    def times(weight, i):
        return jnp.dot(pns[i % 2], weight[...], preferred_element_type=jnp.float32).astype(
            jnp.bfloat16
        )

    waits[0][0].wait()
    pns[0] = normed(0)
    for i in range(blocks):
        rows = pl.ds(base + i * block, block)
        if i == 0:
            waits[0][1].wait()
        ks[rows, :] = times(wk, i)
        if keys_ready is not None:
            keys_ready()
        if i == 0:
            waits[0][2].wait()
        if i + 1 < blocks:
            waits[i + 1][0].wait()
            pns[(i + 1) % 2] = normed(i + 1)
        vs[rows, :] = times(wv, i)


def early_kernel(
    x_hbm, gain_hbm, wk_hbm, wv_hbm, k_hbm, v_hbm, gain_ref, xs, wk, wv, ks, vs, pns, sem
):
    gain_copy = pltpu.make_async_copy(gain_hbm, gain_ref, sem.at[3])
    fetches = [
        pltpu.make_async_copy(x_hbm.at[pl.ds(0, xs.shape[0])], xs, sem.at[0]),
        pltpu.make_async_copy(wk_hbm, wk, sem.at[1]),
        pltpu.make_async_copy(wv_hbm, wv, sem.at[2]),
    ]
    gain_copy.start()
    for fetch in fetches:
        fetch.start()
    key_put = pltpu.make_async_copy(ks, k_hbm, sem.at[4])
    value_put = pltpu.make_async_copy(vs, v_hbm, sem.at[5])
    gain_copy.wait()
    project_rows(
        lambda i: xs[...], gain_ref, wk, wv, ks, vs, pns, [fetches], 0, key_put.start
    )
    value_put.start()
    key_put.wait()
    value_put.wait()


def early(patches, gain, w_key, w_value, block):
    width = patches.shape[1]
    hbm = pl.BlockSpec(memory_space=pltpu.HBM)
    return pl.pallas_call(
        early_kernel,
        in_specs=[hbm] * 4,
        out_specs=[hbm] * 2,
        out_shape=[pltpu.HBM((block, width), jnp.bfloat16)] * 2,
        scratch_shapes=[
            pltpu.VMEM((1, width), jnp.float32),
            pltpu.VMEM((block, width), jnp.bfloat16),
            pltpu.VMEM((width, width), jnp.bfloat16),
            pltpu.VMEM((width, width), jnp.bfloat16),
            pltpu.VMEM((block, width), jnp.bfloat16),
            pltpu.VMEM((block, width), jnp.bfloat16),
            pltpu.VMEM((1, block, width), jnp.bfloat16),
            pltpu.SemaphoreType.DMA((6,)),
        ],
        compiler_params=pltpu.CompilerParams(vmem_limit_bytes=24 * MIB),
        cost_estimate=pl.CostEstimate(
            flops=4 * block * width * width,
            transcendentals=block,
            bytes_accessed=6 * block * width + 4 * width * width,
        ),
        name="early",
    )(in_hbm(patches), in_hbm(gain.reshape(1, width)), in_hbm(w_key), in_hbm(w_value))


def attend_kernel(
    lat_ref,
    lat_gain_ref,
    wq_hbm,
    x_hbm,
    gain_hbm,
    wk_hbm,
    wv_hbm,
    k_hbm,
    v_hbm,
    out_ref,
    gain_ref,
    xs,
    wk,
    wv,
    wq,
    ks,
    vs,
    pns,
    x_sem,
    w_sem,
):
    latents, width = lat_ref.shape
    blocks, block, _ = xs.shape
    rows = ks.shape[0]
    head_dim = width // HEADS
    span = PACK * head_dim
    groups = HEADS // PACK
    fetches = [
        pltpu.make_async_copy(x_hbm.at[pl.ds((i + 1) * block, block)], xs.at[i], x_sem.at[i])
        for i in range(blocks)
    ]
    key_copy = pltpu.make_async_copy(wk_hbm, wk, w_sem.at[0])
    value_copy = pltpu.make_async_copy(wv_hbm, wv, w_sem.at[1])
    later = [
        pltpu.make_async_copy(wq_hbm, wq, w_sem.at[2]),
        pltpu.make_async_copy(k_hbm, ks.at[pl.ds(0, block)], w_sem.at[3]),
        pltpu.make_async_copy(v_hbm, vs.at[pl.ds(0, block)], w_sem.at[4]),
    ]
    gain_copy = pltpu.make_async_copy(gain_hbm, gain_ref, w_sem.at[5])
    gain_copy.start()
    fetches[0].start()
    key_copy.start()
    value_copy.start()
    for fetch in fetches[1:] + later:
        fetch.start()
    lat_norm = norm_rows(lat_ref[...].astype(jnp.float32), lat_gain_ref[...]).astype(jnp.bfloat16)
    gain_copy.wait()
    waits = [(fetches[0], key_copy, value_copy)] + [(fetch,) for fetch in fetches[1:]]
    project_rows(lambda i: xs[i], gain_ref, wk, wv, ks, vs, pns, waits, block)
    for fetch in later:
        fetch.wait()
    query = jnp.dot(lat_norm, wq[...], preferred_element_type=jnp.float32).astype(jnp.bfloat16)

    lane_head = lax.broadcasted_iota(jnp.int32, (latents, span), 1) // head_dim
    lane = lax.broadcasted_iota(jnp.int32, (latents, LANES), 1)
    factor = math.log2(math.e) / math.sqrt(head_dim)
    piece = rows if PACK * latents <= 512 else block
    out = jnp.zeros((latents, LANES), jnp.float32)
    for g in range(groups):
        cols = slice(g * span, (g + 1) * span)
        part = query[:, cols]
        apart = jnp.concatenate(
            [jnp.where(lane_head == h, part, jnp.zeros_like(part)) for h in range(PACK)], axis=0
        )
        total = numer = None
        for start in range(0, rows, piece):
            scores = lax.dot_general(
                apart,
                ks[start : start + piece, cols],
                (((1,), (1,)), ((), ())),
                preferred_element_type=jnp.float32,
            )
            expo = jnp.exp2(scores * factor)
            for j in range(piece // LANES):
                lanes = expo[:, j * LANES : (j + 1) * LANES]
                total = lanes if total is None else total + lanes
            here = jnp.dot(
                expo.astype(jnp.bfloat16),
                vs[start : start + piece, cols],
                preferred_element_type=jnp.float32,
            )
            numer = here if numer is None else numer + here
        sums = jnp.sum(total, axis=-1, keepdims=True)
        high = sums.astype(jnp.bfloat16).astype(jnp.float32)
        low = sums - high
        picked = jnp.zeros((latents, span), jnp.float32)
        for h in range(PACK):
            mine = slice(h * latents, (h + 1) * latents)
            picked = jnp.where(lane_head == h, numer[mine], picked)
            out = jnp.where(lane == g * PACK + h, high[mine], out)
            out = jnp.where(lane == HEADS + g * PACK + h, low[mine], out)
        out_ref[:, cols] = picked.astype(jnp.bfloat16)
    out_ref[:, width:] = out.astype(jnp.bfloat16)


def attend(latents, lat_gain, w_query, patches, gain, w_key, w_value, keys, values):
    rows, width = patches.shape
    block = keys.shape[0]
    blocks = rows // block - 1
    count = latents.shape[0]
    vmem = pl.BlockSpec(memory_space=pltpu.VMEM)
    hbm = pl.BlockSpec(memory_space=pltpu.HBM)
    return pl.pallas_call(
        attend_kernel,
        in_specs=[vmem, vmem] + [hbm] * 7,
        out_specs=vmem,
        out_shape=jax.ShapeDtypeStruct((count, width + LANES), jnp.bfloat16),
        scratch_shapes=[
            pltpu.VMEM((1, width), jnp.float32),
            pltpu.VMEM((blocks, block, width), jnp.bfloat16),
            pltpu.VMEM((width, width), jnp.bfloat16),
            pltpu.VMEM((width, width), jnp.bfloat16),
            pltpu.VMEM((width, width), jnp.bfloat16),
            pltpu.VMEM((rows, width), jnp.bfloat16),
            pltpu.VMEM((rows, width), jnp.bfloat16),
            pltpu.VMEM((2, block, width), jnp.bfloat16),
            pltpu.SemaphoreType.DMA((blocks,)),
            pltpu.SemaphoreType.DMA((6,)),
        ],
        compiler_params=pltpu.CompilerParams(vmem_limit_bytes=42 * MIB),
        cost_estimate=pl.CostEstimate(
            flops=4 * (rows - block) * width * width + 4 * rows * count * PACK * width,
            transcendentals=rows * count * HEADS,
            bytes_accessed=2 * rows * width + 6 * width * width,
        ),
        name="attend",
    )(
        latents,
        lat_gain.reshape(1, width),
        in_hbm(w_query),
        in_hbm(patches),
        in_hbm(gain.reshape(1, width)),
        in_hbm(w_key),
        in_hbm(w_value),
        in_hbm(keys),
        in_hbm(values),
    )


def exchange(blocks):
    return lax.all_to_all(blocks, "page", 0, 0, tiled=True)


def spread(block, count):
    return jnp.broadcast_to(block[None], (count,) + block.shape)


def exchange_side(blocks, count):
    sides = [[2 * chip + side for chip in range(count // 2)] for side in range(2)]
    return lax.all_to_all(blocks, "page", 0, 0, axis_index_groups=sides, tiled=True)


def swap_cores(array, count):
    return lax.ppermute(array, "page", [(i, i ^ 1) for i in range(count)])


def by_side(even, mine, theirs, axis):
    return jnp.concatenate([jnp.where(even, mine, theirs), jnp.where(even, theirs, mine)], axis=axis)


def body(
    latents,
    patches,
    lat_gain,
    patch_gain,
    mlp_gain,
    w_query,
    w_key,
    w_value,
    w_out,
    w_hidden,
    w_connect,
):
    count = lax.axis_size("page")
    lat_rows, width = latents.shape
    lat_all = exchange(spread(latents, count)).reshape(count * lat_rows, width)
    block = math.gcd(patches.shape[0], BLOCK)
    keys, values = early(patches, patch_gain, w_key, w_value, block)
    even = lax.axis_index("page") % 2 == 0
    lat_all, w_theirs, even = lax.optimization_barrier(
        (lat_all, swap_cores(w_hidden, count), even)
    )
    packed = attend(
        lat_all, lat_gain, w_query, patches, patch_gain, w_key, w_value, keys, values
    )
    parts = exchange(packed.reshape(count, lat_rows, width + LANES))
    summed = jnp.sum(parts.astype(jnp.float32), axis=0)
    denom = summed[:, width : width + HEADS] + summed[:, width + HEADS : width + 2 * HEADS]
    attended = (
        (summed[:, :width].reshape(lat_rows, HEADS, width // HEADS) / denom[:, :, None])
        .reshape(lat_rows, width)
        .astype(jnp.bfloat16)
    )
    mixed = latents.astype(jnp.float32) + jnp.dot(
        attended, w_out, preferred_element_type=jnp.float32
    )
    resampled = mixed.astype(jnp.bfloat16)
    mlp_in = norm_rows(mixed, mlp_gain).astype(jnp.bfloat16)
    chips = count // 2
    rows = chips * lat_rows
    mlp_side = exchange_side(spread(mlp_in, chips), count).reshape(rows, width)

    def hidden_of(weight):
        return jax.nn.gelu(
            jnp.dot(mlp_side, weight, preferred_element_type=jnp.float32), approximate=True
        ).astype(jnp.bfloat16)

    hidden = by_side(even, hidden_of(w_hidden), hidden_of(w_theirs), 1)
    hidden_mine = exchange_side(spread(hidden, chips), count)
    hidden_theirs = swap_cores(hidden_mine, count)

    def connect(blocks):
        flat = jnp.transpose(blocks, (1, 0, 2)).reshape(rows, w_connect.shape[0])
        return jnp.dot(flat, w_connect, preferred_element_type=jnp.float32).astype(jnp.bfloat16)

    sides = [
        part.reshape(chips, 1, lat_rows, w_connect.shape[1])
        for part in (connect(hidden_mine), connect(hidden_theirs))
    ]
    connector = by_side(even, sides[0], sides[1], 1).reshape(count * lat_rows, w_connect.shape[1])
    return (resampled, connector)


def solution(mesh):
    placed = (
        P(("slab", "page"), None),
        P(("slab", "page"), None),
        P(),
        P(),
        P(),
        P(),
        P(),
        P(),
        P(),
        P(None, "page"),
        P(None, "page"),
    )
    return jax.shard_map(
        body,
        mesh=mesh,
        in_specs=placed,
        out_specs=(P(("slab", "page"), None), P("slab", "page")),
        check_vma=False,
    )
```

```python
import math

import jax
import jax.numpy as jnp
from jax import lax
from jax.experimental import pallas as pl
from jax.experimental.pallas import tpu as pltpu
from jax.sharding import PartitionSpec as P

HEADS = 16
PACK = 4
LANES = 128
BLOCK = 512
MIB = 1024 * 1024


def norm_rows(values_in, gain):
    center = values_in - jnp.mean(values_in, axis=-1, keepdims=True)
    spread = jnp.mean(center * center, axis=-1, keepdims=True)
    return center * lax.rsqrt(spread + 1e-05) * gain


def in_hbm(array):
    return pltpu.with_memory_space_constraint(array, pltpu.HBM)


def project_rows(get, gain_ref, wk, wv, ks, vs, pns, waits, base, keys_ready=None):
    blocks = len(waits)
    block = pns.shape[1]

    def normed(i):
        return norm_rows(get(i).astype(jnp.float32), gain_ref[...]).astype(jnp.bfloat16)

    def times(weight, i):
        return jnp.dot(pns[i % 2], weight[...], preferred_element_type=jnp.float32).astype(
            jnp.bfloat16
        )

    waits[0][0].wait()
    pns[0] = normed(0)
    for i in range(blocks):
        rows = pl.ds(base + i * block, block)
        if i == 0:
            waits[0][1].wait()
        ks[rows, :] = times(wk, i)
        if keys_ready is not None:
            keys_ready()
        if i == 0:
            waits[0][2].wait()
        if i + 1 < blocks:
            waits[i + 1][0].wait()
            pns[(i + 1) % 2] = normed(i + 1)
        vs[rows, :] = times(wv, i)


def early_kernel(
    x_hbm, gain_hbm, wk_hbm, wv_hbm, k_hbm, v_hbm, gain_ref, xs, wk, wv, ks, vs, pns, sem
):
    gain_copy = pltpu.make_async_copy(gain_hbm, gain_ref, sem.at[3])
    fetches = [
        pltpu.make_async_copy(x_hbm.at[pl.ds(0, xs.shape[0])], xs, sem.at[0]),
        pltpu.make_async_copy(wk_hbm, wk, sem.at[1]),
        pltpu.make_async_copy(wv_hbm, wv, sem.at[2]),
    ]
    gain_copy.start()
    for fetch in fetches:
        fetch.start()
    key_put = pltpu.make_async_copy(ks, k_hbm, sem.at[4])
    value_put = pltpu.make_async_copy(vs, v_hbm, sem.at[5])
    gain_copy.wait()
    project_rows(
        lambda i: xs[...], gain_ref, wk, wv, ks, vs, pns, [fetches], 0, key_put.start
    )
    value_put.start()
    key_put.wait()
    value_put.wait()


def early(patches, gain, w_key, w_value, block):
    width = patches.shape[1]
    hbm = pl.BlockSpec(memory_space=pltpu.HBM)
    return pl.pallas_call(
        early_kernel,
        in_specs=[hbm] * 4,
        out_specs=[hbm] * 2,
        out_shape=[pltpu.HBM((block, width), jnp.bfloat16)] * 2,
        scratch_shapes=[
            pltpu.VMEM((1, width), jnp.float32),
            pltpu.VMEM((block, width), jnp.bfloat16),
            pltpu.VMEM((width, width), jnp.bfloat16),
            pltpu.VMEM((width, width), jnp.bfloat16),
            pltpu.VMEM((block, width), jnp.bfloat16),
            pltpu.VMEM((block, width), jnp.bfloat16),
            pltpu.VMEM((1, block, width), jnp.bfloat16),
            pltpu.SemaphoreType.DMA((6,)),
        ],
        compiler_params=pltpu.CompilerParams(vmem_limit_bytes=24 * MIB),
        cost_estimate=pl.CostEstimate(
            flops=4 * block * width * width,
            transcendentals=block,
            bytes_accessed=6 * block * width + 4 * width * width,
        ),
        name="early",
    )(in_hbm(patches), in_hbm(gain.reshape(1, width)), in_hbm(w_key), in_hbm(w_value))


def attend_kernel(
    lat_ref,
    lat_gain_ref,
    wq_hbm,
    x_hbm,
    gain_hbm,
    wk_hbm,
    wv_hbm,
    k_hbm,
    v_hbm,
    out_ref,
    gain_ref,
    xs,
    wk,
    wv,
    wq,
    ks,
    vs,
    pns,
    x_sem,
    w_sem,
):
    latents, width = lat_ref.shape
    blocks, block, _ = xs.shape
    rows = ks.shape[0]
    head_dim = width // HEADS
    span = PACK * head_dim
    groups = HEADS // PACK
    fetches = [
        pltpu.make_async_copy(x_hbm.at[pl.ds((i + 1) * block, block)], xs.at[i], x_sem.at[i])
        for i in range(blocks)
    ]
    key_copy = pltpu.make_async_copy(wk_hbm, wk, w_sem.at[0])
    value_copy = pltpu.make_async_copy(wv_hbm, wv, w_sem.at[1])
    later = [
        pltpu.make_async_copy(wq_hbm, wq, w_sem.at[2]),
        pltpu.make_async_copy(k_hbm, ks.at[pl.ds(0, block)], w_sem.at[3]),
        pltpu.make_async_copy(v_hbm, vs.at[pl.ds(0, block)], w_sem.at[4]),
    ]
    gain_copy = pltpu.make_async_copy(gain_hbm, gain_ref, w_sem.at[5])
    gain_copy.start()
    fetches[0].start()
    key_copy.start()
    value_copy.start()
    for fetch in fetches[1:] + later:
        fetch.start()
    lat_norm = norm_rows(lat_ref[...].astype(jnp.float32), lat_gain_ref[...]).astype(jnp.bfloat16)
    gain_copy.wait()
    waits = [(fetches[0], key_copy, value_copy)] + [(fetch,) for fetch in fetches[1:]]
    project_rows(lambda i: xs[i], gain_ref, wk, wv, ks, vs, pns, waits, block)
    for fetch in later:
        fetch.wait()
    query = jnp.dot(lat_norm, wq[...], preferred_element_type=jnp.float32).astype(jnp.bfloat16)

    lane_head = lax.broadcasted_iota(jnp.int32, (latents, span), 1) // head_dim
    lane = lax.broadcasted_iota(jnp.int32, (latents, LANES), 1)
    factor = math.log2(math.e) / math.sqrt(head_dim)
    piece = rows if PACK * latents <= 512 else block
    out = jnp.zeros((latents, LANES), jnp.float32)
    for g in range(groups):
        cols = slice(g * span, (g + 1) * span)
        part = query[:, cols]
        apart = jnp.concatenate(
            [jnp.where(lane_head == h, part, jnp.zeros_like(part)) for h in range(PACK)], axis=0
        )
        total = numer = None
        for start in range(0, rows, piece):
            scores = lax.dot_general(
                apart,
                ks[start : start + piece, cols],
                (((1,), (1,)), ((), ())),
                preferred_element_type=jnp.float32,
            )
            expo = jnp.exp2(scores * factor)
            for j in range(piece // LANES):
                lanes = expo[:, j * LANES : (j + 1) * LANES]
                total = lanes if total is None else total + lanes
            here = jnp.dot(
                expo.astype(jnp.bfloat16),
                vs[start : start + piece, cols],
                preferred_element_type=jnp.float32,
            )
            numer = here if numer is None else numer + here
        sums = jnp.sum(total, axis=-1, keepdims=True)
        high = sums.astype(jnp.bfloat16).astype(jnp.float32)
        low = sums - high
        picked = jnp.zeros((latents, span), jnp.float32)
        for h in range(PACK):
            mine = slice(h * latents, (h + 1) * latents)
            picked = jnp.where(lane_head == h, numer[mine], picked)
            out = jnp.where(lane == g * PACK + h, high[mine], out)
            out = jnp.where(lane == HEADS + g * PACK + h, low[mine], out)
        out_ref[:, cols] = picked.astype(jnp.bfloat16)
    out_ref[:, width:] = out.astype(jnp.bfloat16)


def attend(latents, lat_gain, w_query, patches, gain, w_key, w_value, keys, values):
    rows, width = patches.shape
    block = keys.shape[0]
    blocks = rows // block - 1
    count = latents.shape[0]
    vmem = pl.BlockSpec(memory_space=pltpu.VMEM)
    hbm = pl.BlockSpec(memory_space=pltpu.HBM)
    return pl.pallas_call(
        attend_kernel,
        in_specs=[vmem, vmem] + [hbm] * 7,
        out_specs=vmem,
        out_shape=jax.ShapeDtypeStruct((count, width + LANES), jnp.bfloat16),
        scratch_shapes=[
            pltpu.VMEM((1, width), jnp.float32),
            pltpu.VMEM((blocks, block, width), jnp.bfloat16),
            pltpu.VMEM((width, width), jnp.bfloat16),
            pltpu.VMEM((width, width), jnp.bfloat16),
            pltpu.VMEM((width, width), jnp.bfloat16),
            pltpu.VMEM((rows, width), jnp.bfloat16),
            pltpu.VMEM((rows, width), jnp.bfloat16),
            pltpu.VMEM((2, block, width), jnp.bfloat16),
            pltpu.SemaphoreType.DMA((blocks,)),
            pltpu.SemaphoreType.DMA((6,)),
        ],
        compiler_params=pltpu.CompilerParams(vmem_limit_bytes=42 * MIB),
        cost_estimate=pl.CostEstimate(
            flops=4 * (rows - block) * width * width + 4 * rows * count * PACK * width,
            transcendentals=rows * count * HEADS,
            bytes_accessed=2 * rows * width + 6 * width * width,
        ),
        name="attend",
    )(
        latents,
        lat_gain.reshape(1, width),
        in_hbm(w_query),
        in_hbm(patches),
        in_hbm(gain.reshape(1, width)),
        in_hbm(w_key),
        in_hbm(w_value),
        in_hbm(keys),
        in_hbm(values),
    )


def exchange(blocks):
    return lax.all_to_all(blocks, "page", 0, 0, tiled=True)


def spread(block, count):
    return jnp.broadcast_to(block[None], (count,) + block.shape)


def exchange_side(blocks, count):
    sides = [[2 * chip + side for chip in range(count // 2)] for side in range(2)]
    return lax.all_to_all(blocks, "page", 0, 0, axis_index_groups=sides, tiled=True)


def swap_cores(array, count):
    return lax.ppermute(array, "page", [(i, i ^ 1) for i in range(count)])


def by_side(even, mine, theirs, axis):
    return jnp.concatenate([jnp.where(even, mine, theirs), jnp.where(even, theirs, mine)], axis=axis)


def body(
    latents,
    patches,
    lat_gain,
    patch_gain,
    mlp_gain,
    w_query,
    w_key,
    w_value,
    w_out,
    w_hidden,
    w_connect,
):
    count = lax.axis_size("page")
    lat_rows, width = latents.shape
    lat_all = exchange(spread(latents, count)).reshape(count * lat_rows, width)
    block = math.gcd(patches.shape[0], BLOCK)
    keys, values = early(patches, patch_gain, w_key, w_value, block)
    even = lax.axis_index("page") % 2 == 0
    lat_all, w_theirs, even = lax.optimization_barrier(
        (lat_all, swap_cores(w_hidden, count), even)
    )
    packed = attend(
        lat_all, lat_gain, w_query, patches, patch_gain, w_key, w_value, keys, values
    )
    chips = count // 2
    packed = packed.reshape(chips, 2, lat_rows, width + LANES)
    keep = jnp.where(even, packed[:, 0], packed[:, 1])
    give = jnp.where(even, packed[:, 1], packed[:, 0])
    pair = keep.astype(jnp.float32) + swap_cores(give, count).astype(jnp.float32)
    parts = exchange_side(pair.astype(jnp.bfloat16), count)
    summed = jnp.sum(parts.astype(jnp.float32), axis=0)
    denom = summed[:, width : width + HEADS] + summed[:, width + HEADS : width + 2 * HEADS]
    attended = (
        (summed[:, :width].reshape(lat_rows, HEADS, width // HEADS) / denom[:, :, None])
        .reshape(lat_rows, width)
        .astype(jnp.bfloat16)
    )
    mixed = latents.astype(jnp.float32) + jnp.dot(
        attended, w_out, preferred_element_type=jnp.float32
    )
    resampled = mixed.astype(jnp.bfloat16)
    mlp_in = norm_rows(mixed, mlp_gain).astype(jnp.bfloat16)
    rows = chips * lat_rows
    mlp_side = exchange_side(spread(mlp_in, chips), count).reshape(rows, width)

    def hidden_of(weight):
        return jax.nn.gelu(
            jnp.dot(mlp_side, weight, preferred_element_type=jnp.float32), approximate=True
        ).astype(jnp.bfloat16)

    hidden = by_side(even, hidden_of(w_hidden), hidden_of(w_theirs), 1)
    hidden_mine = exchange_side(spread(hidden, chips), count)
    hidden_theirs = swap_cores(hidden_mine, count)

    def connect(blocks):
        flat = jnp.transpose(blocks, (1, 0, 2)).reshape(rows, w_connect.shape[0])
        return jnp.dot(flat, w_connect, preferred_element_type=jnp.float32).astype(jnp.bfloat16)

    sides = [
        part.reshape(chips, 1, lat_rows, w_connect.shape[1])
        for part in (connect(hidden_mine), connect(hidden_theirs))
    ]
    connector = by_side(even, sides[0], sides[1], 1).reshape(count * lat_rows, w_connect.shape[1])
    return (resampled, connector)


def solution(mesh):
    placed = (
        P(("slab", "page"), None),
        P(("slab", "page"), None),
        P(),
        P(),
        P(),
        P(),
        P(),
        P(),
        P(),
        P(None, "page"),
        P(None, "page"),
    )
    return jax.shard_map(
        body,
        mesh=mesh,
        in_specs=placed,
        out_specs=(P(("slab", "page"), None), P("slab", "page")),
        check_vma=False,
    )
```

```python
import math

import jax
import jax.numpy as jnp
from jax import lax
from jax.experimental import pallas as pl
from jax.experimental.pallas import tpu as pltpu
from jax.sharding import PartitionSpec as P

HEADS = 16
PACK = 4
LANES = 128
BLOCK = 512
MIB = 1024 * 1024


def norm_rows(values_in, gain):
    center = values_in - jnp.mean(values_in, axis=-1, keepdims=True)
    spread = jnp.mean(center * center, axis=-1, keepdims=True)
    return center * lax.rsqrt(spread + 1e-05) * gain


def in_hbm(array):
    return pltpu.with_memory_space_constraint(array, pltpu.HBM)


def project_rows(get, gain_ref, wk, wv, ks, vs, pns, waits, base, keys_ready=None):
    blocks = len(waits)
    block = pns.shape[1]

    def normed(i):
        return norm_rows(get(i).astype(jnp.float32), gain_ref[...]).astype(jnp.bfloat16)

    def times(weight, i):
        return jnp.dot(pns[i % 2], weight[...], preferred_element_type=jnp.float32).astype(
            jnp.bfloat16
        )

    waits[0][0].wait()
    pns[0] = normed(0)
    for i in range(blocks):
        rows = pl.ds(base + i * block, block)
        if i == 0:
            waits[0][1].wait()
        ks[rows, :] = times(wk, i)
        if keys_ready is not None:
            keys_ready()
        if i == 0:
            waits[0][2].wait()
        if i + 1 < blocks:
            waits[i + 1][0].wait()
            pns[(i + 1) % 2] = normed(i + 1)
        vs[rows, :] = times(wv, i)


def early_kernel(
    x_hbm, gain_hbm, wk_hbm, wv_hbm, k_hbm, v_hbm, gain_ref, xs, wk, wv, ks, vs, pns, sem
):
    gain_copy = pltpu.make_async_copy(gain_hbm, gain_ref, sem.at[3])
    fetches = [
        pltpu.make_async_copy(x_hbm.at[pl.ds(0, xs.shape[0])], xs, sem.at[0]),
        pltpu.make_async_copy(wk_hbm, wk, sem.at[1]),
        pltpu.make_async_copy(wv_hbm, wv, sem.at[2]),
    ]
    gain_copy.start()
    for fetch in fetches:
        fetch.start()
    key_put = pltpu.make_async_copy(ks, k_hbm, sem.at[4])
    value_put = pltpu.make_async_copy(vs, v_hbm, sem.at[5])
    gain_copy.wait()
    project_rows(
        lambda i: xs[...], gain_ref, wk, wv, ks, vs, pns, [fetches], 0, key_put.start
    )
    value_put.start()
    key_put.wait()
    value_put.wait()


def early(patches, gain, w_key, w_value, block):
    width = patches.shape[1]
    hbm = pl.BlockSpec(memory_space=pltpu.HBM)
    return pl.pallas_call(
        early_kernel,
        in_specs=[hbm] * 4,
        out_specs=[hbm] * 2,
        out_shape=[pltpu.HBM((block, width), jnp.bfloat16)] * 2,
        scratch_shapes=[
            pltpu.VMEM((1, width), jnp.float32),
            pltpu.VMEM((block, width), jnp.bfloat16),
            pltpu.VMEM((width, width), jnp.bfloat16),
            pltpu.VMEM((width, width), jnp.bfloat16),
            pltpu.VMEM((block, width), jnp.bfloat16),
            pltpu.VMEM((block, width), jnp.bfloat16),
            pltpu.VMEM((1, block, width), jnp.bfloat16),
            pltpu.SemaphoreType.DMA((6,)),
        ],
        compiler_params=pltpu.CompilerParams(vmem_limit_bytes=24 * MIB),
        cost_estimate=pl.CostEstimate(
            flops=4 * block * width * width,
            transcendentals=block,
            bytes_accessed=6 * block * width + 4 * width * width,
        ),
        name="early",
    )(in_hbm(patches), in_hbm(gain.reshape(1, width)), in_hbm(w_key), in_hbm(w_value))


def attend_kernel(
    lat_ref,
    lat_gain_ref,
    wq_hbm,
    x_hbm,
    gain_hbm,
    wk_hbm,
    wv_hbm,
    k_hbm,
    v_hbm,
    out_ref,
    gain_ref,
    xs,
    wk,
    wv,
    wq,
    ks,
    vs,
    pns,
    x_sem,
    w_sem,
):
    latents, width = lat_ref.shape
    blocks, block, _ = xs.shape
    rows = ks.shape[0]
    head_dim = width // HEADS
    span = PACK * head_dim
    groups = HEADS // PACK
    fetches = [
        pltpu.make_async_copy(x_hbm.at[pl.ds((i + 1) * block, block)], xs.at[i], x_sem.at[i])
        for i in range(blocks)
    ]
    key_copy = pltpu.make_async_copy(wk_hbm, wk, w_sem.at[0])
    value_copy = pltpu.make_async_copy(wv_hbm, wv, w_sem.at[1])
    later = [
        pltpu.make_async_copy(wq_hbm, wq, w_sem.at[2]),
        pltpu.make_async_copy(k_hbm, ks.at[pl.ds(0, block)], w_sem.at[3]),
        pltpu.make_async_copy(v_hbm, vs.at[pl.ds(0, block)], w_sem.at[4]),
    ]
    gain_copy = pltpu.make_async_copy(gain_hbm, gain_ref, w_sem.at[5])
    gain_copy.start()
    fetches[0].start()
    key_copy.start()
    value_copy.start()
    for fetch in fetches[1:] + later:
        fetch.start()
    lat_norm = norm_rows(lat_ref[...].astype(jnp.float32), lat_gain_ref[...]).astype(jnp.bfloat16)
    gain_copy.wait()
    waits = [(fetches[0], key_copy, value_copy)] + [(fetch,) for fetch in fetches[1:]]
    project_rows(lambda i: xs[i], gain_ref, wk, wv, ks, vs, pns, waits, block)
    for fetch in later:
        fetch.wait()
    query = jnp.dot(lat_norm, wq[...], preferred_element_type=jnp.float32).astype(jnp.bfloat16)

    lane_head = lax.broadcasted_iota(jnp.int32, (latents, span), 1) // head_dim
    lane = lax.broadcasted_iota(jnp.int32, (latents, LANES), 1)
    factor = math.log2(math.e) / math.sqrt(head_dim)
    piece = rows if PACK * latents <= 512 else block
    out = jnp.zeros((latents, LANES), jnp.float32)
    for g in range(groups):
        cols = slice(g * span, (g + 1) * span)
        part = query[:, cols]
        apart = jnp.concatenate(
            [jnp.where(lane_head == h, part, jnp.zeros_like(part)) for h in range(PACK)], axis=0
        )
        total = numer = None
        for start in range(0, rows, piece):
            scores = lax.dot_general(
                apart,
                ks[start : start + piece, cols],
                (((1,), (1,)), ((), ())),
                preferred_element_type=jnp.float32,
            )
            expo = jnp.exp2(scores * factor)
            for j in range(piece // LANES):
                lanes = expo[:, j * LANES : (j + 1) * LANES]
                total = lanes if total is None else total + lanes
            here = jnp.dot(
                expo.astype(jnp.bfloat16),
                vs[start : start + piece, cols],
                preferred_element_type=jnp.float32,
            )
            numer = here if numer is None else numer + here
        sums = jnp.sum(total, axis=-1, keepdims=True)
        high = sums.astype(jnp.bfloat16).astype(jnp.float32)
        low = sums - high
        picked = jnp.zeros((latents, span), jnp.float32)
        for h in range(PACK):
            mine = slice(h * latents, (h + 1) * latents)
            picked = jnp.where(lane_head == h, numer[mine], picked)
            out = jnp.where(lane == g * PACK + h, high[mine], out)
            out = jnp.where(lane == HEADS + g * PACK + h, low[mine], out)
        out_ref[:, cols] = picked.astype(jnp.bfloat16)
    out_ref[:, width:] = out.astype(jnp.bfloat16)


def attend(latents, lat_gain, w_query, patches, gain, w_key, w_value, keys, values):
    rows, width = patches.shape
    block = keys.shape[0]
    blocks = rows // block - 1
    count = latents.shape[0]
    vmem = pl.BlockSpec(memory_space=pltpu.VMEM)
    hbm = pl.BlockSpec(memory_space=pltpu.HBM)
    return pl.pallas_call(
        attend_kernel,
        in_specs=[vmem, vmem] + [hbm] * 7,
        out_specs=vmem,
        out_shape=jax.ShapeDtypeStruct((count, width + LANES), jnp.bfloat16),
        scratch_shapes=[
            pltpu.VMEM((1, width), jnp.float32),
            pltpu.VMEM((blocks, block, width), jnp.bfloat16),
            pltpu.VMEM((width, width), jnp.bfloat16),
            pltpu.VMEM((width, width), jnp.bfloat16),
            pltpu.VMEM((width, width), jnp.bfloat16),
            pltpu.VMEM((rows, width), jnp.bfloat16),
            pltpu.VMEM((rows, width), jnp.bfloat16),
            pltpu.VMEM((2, block, width), jnp.bfloat16),
            pltpu.SemaphoreType.DMA((blocks,)),
            pltpu.SemaphoreType.DMA((6,)),
        ],
        compiler_params=pltpu.CompilerParams(vmem_limit_bytes=42 * MIB),
        cost_estimate=pl.CostEstimate(
            flops=4 * (rows - block) * width * width + 4 * rows * count * PACK * width,
            transcendentals=rows * count * HEADS,
            bytes_accessed=2 * rows * width + 6 * width * width,
        ),
        name="attend",
    )(
        latents,
        lat_gain.reshape(1, width),
        in_hbm(w_query),
        in_hbm(patches),
        in_hbm(gain.reshape(1, width)),
        in_hbm(w_key),
        in_hbm(w_value),
        in_hbm(keys),
        in_hbm(values),
    )


def exchange(blocks):
    return lax.all_to_all(blocks, "page", 0, 0, tiled=True)


def spread(block, count):
    return jnp.broadcast_to(block[None], (count,) + block.shape)


def exchange_side(blocks, count):
    sides = [[2 * chip + side for chip in range(count // 2)] for side in range(2)]
    return lax.all_to_all(blocks, "page", 0, 0, axis_index_groups=sides, tiled=True)


def swap_cores(array, count):
    return lax.ppermute(array, "page", [(i, i ^ 1) for i in range(count)])


def by_side(even, mine, theirs, axis):
    return jnp.concatenate([jnp.where(even, mine, theirs), jnp.where(even, theirs, mine)], axis=axis)


def body(
    latents,
    patches,
    lat_gain,
    patch_gain,
    mlp_gain,
    w_query,
    w_key,
    w_value,
    w_out,
    w_hidden,
    w_connect,
):
    count = lax.axis_size("page")
    lat_rows, width = latents.shape
    lat_all = exchange(spread(latents, count)).reshape(count * lat_rows, width)
    block = math.gcd(patches.shape[0], BLOCK)
    keys, values = early(patches, patch_gain, w_key, w_value, block)
    even = lax.axis_index("page") % 2 == 0
    lat_all, even = lax.optimization_barrier((lat_all, even))
    packed = attend(
        lat_all, lat_gain, w_query, patches, patch_gain, w_key, w_value, keys, values
    )
    chips = count // 2
    packed = packed.reshape(chips, 2, lat_rows, width + LANES)
    keep = jnp.where(even, packed[:, 0], packed[:, 1])
    give = jnp.where(even, packed[:, 1], packed[:, 0])
    give, w_give = lax.optimization_barrier((give, w_hidden))
    got, w_theirs = lax.optimization_barrier((swap_cores(give, count), swap_cores(w_give, count)))
    pair = keep.astype(jnp.float32) + got.astype(jnp.float32)
    parts = exchange_side(pair.astype(jnp.bfloat16), count)
    summed = jnp.sum(parts.astype(jnp.float32), axis=0)
    denom = summed[:, width : width + HEADS] + summed[:, width + HEADS : width + 2 * HEADS]
    attended = (
        (summed[:, :width].reshape(lat_rows, HEADS, width // HEADS) / denom[:, :, None])
        .reshape(lat_rows, width)
        .astype(jnp.bfloat16)
    )
    mixed = latents.astype(jnp.float32) + jnp.dot(
        attended, w_out, preferred_element_type=jnp.float32
    )
    resampled = mixed.astype(jnp.bfloat16)
    mlp_in = norm_rows(mixed, mlp_gain).astype(jnp.bfloat16)
    rows = chips * lat_rows
    mlp_side = exchange_side(spread(mlp_in, chips), count).reshape(rows, width)

    def hidden_of(weight):
        return jax.nn.gelu(
            jnp.dot(mlp_side, weight, preferred_element_type=jnp.float32), approximate=True
        ).astype(jnp.bfloat16)

    hidden = by_side(even, hidden_of(w_hidden), hidden_of(w_theirs), 1)
    hidden_mine = exchange_side(spread(hidden, chips), count)
    hidden_theirs = swap_cores(hidden_mine, count)

    def connect(blocks):
        flat = jnp.transpose(blocks, (1, 0, 2)).reshape(rows, w_connect.shape[0])
        return jnp.dot(flat, w_connect, preferred_element_type=jnp.float32).astype(jnp.bfloat16)

    sides = [
        part.reshape(chips, 1, lat_rows, w_connect.shape[1])
        for part in (connect(hidden_mine), connect(hidden_theirs))
    ]
    connector = by_side(even, sides[0], sides[1], 1).reshape(count * lat_rows, w_connect.shape[1])
    return (resampled, connector)


def solution(mesh):
    placed = (
        P(("slab", "page"), None),
        P(("slab", "page"), None),
        P(),
        P(),
        P(),
        P(),
        P(),
        P(),
        P(),
        P(None, "page"),
        P(None, "page"),
    )
    return jax.shard_map(
        body,
        mesh=mesh,
        in_specs=placed,
        out_specs=(P(("slab", "page"), None), P("slab", "page")),
        check_vma=False,
    )
```
